32 devices in a mesh: row: 4 (over y, x), col: 8 (over z, core).
Axes of the slice: x: 2, y: 2, z: 4, core: 2. Of those that a mesh axis runs over, the one named last changes fastest.
Arguments:
- alignment: float32 [256, 256, 256], P('row', 'col'), may hold values from -6 to 6
- align_gain: float32 [256], replicated, may hold values from 0.5 to 1.5
- align_bias: float32 [256], replicated, may hold values from -1.75 to 1.75
- left_weight: float32 [256, 32], replicated, may hold values from -0.375 to 0.375
- right_weight: float32 [256, 32], replicated, may hold values from -0.375 to 0.375
- project_weight: float32 [1024, 128], replicated, may hold values from -3 to 3
- project_bias: float32 [128], replicated, may hold values from -1.75 to 1.75
- pair_state: float32 [256, 256, 128], P('row', 'col'), may hold values from -6 to 6
- pair_gain: float32 [128], replicated, may hold values from 0.5 to 1.5
- pair_bias: float32 [128], replicated, may hold values from -1.75 to 1.75
- hidden_weight: float32 [128, 512], replicated, may hold values from -0.5 to 0.5
- hidden_bias: float32 [512], replicated, may hold values from -1.75 to 1.75
- final_weight: float32 [512, 128], replicated, may hold values from -0.25 to 0.25
- final_bias: float32 [128], replicated, may hold values from -1.75 to 1.75
Outputs:
- pair_next: float32 [256, 256, 128], P('row', 'col')
The draws below stay inside these ranges and needn't reach their ends.
All inputs are finite; a program needn't handle non-finite values.
Results may differ from the reference program's by a relative error of at most 0.0003.
Values sent between devices are 32-bit elements; how exact they have to be, the bound alone decides.
No kernel may reach another device: no remote copies, remote signals or barrier semaphores. Data moves between devices by JAX's collectives and lax.ppermute only.
A program may use at most 128 MiB of HBM per device.

```python
import jax
import jax.numpy as jnp
from jax import lax

CM = 256
C = 32
P_SIZE = 128
H = 512
S = 256
R = 256


def shard_levels(key, extent, pieces, least, largest):
    level, own = 1.0, jax.random.fold_in(key, 6)
    for axis_at, blocks in pieces:
        heights = jnp.exp(jax.random.uniform(jax.random.fold_in(own, axis_at), (blocks,), jnp.float32, least / len(pieces), largest / len(pieces)))
        level = level * jnp.repeat(heights, extent[axis_at] // blocks).reshape([-1 if axis == axis_at else 1 for axis in range(len(extent))])
    return level


def noise(key, dims, scale, limit, split=(), held_as=jnp.bfloat16):
    level = shard_levels(key, dims, split, -0.22, 0.18) if split else 1.0
    values = jax.random.normal(key, dims, jnp.float32) * scale * level
    return jnp.minimum(jnp.maximum(values, -limit), limit).astype(held_as)


def setup_inputs(seed: int = 0) -> dict:
    arg_keys = jax.random.split(jax.random.key(seed), 15)
    return {
        "alignment": noise(arg_keys[0], (S, R, CM), 1.0, 6.0, ((0, 4), (1, 8)), jnp.float32),
        "align_gain": jnp.clip(1.0 + 0.1 * jax.random.normal(arg_keys[1], (CM,), jnp.float32), 0.5, 1.5),
        "align_bias": noise(arg_keys[2], (CM,), 0.3, 1.75, (), jnp.float32),
        "left_weight": noise(arg_keys[3], (CM, C), CM ** -0.5, 0.375, (), jnp.float32),
        "right_weight": noise(arg_keys[4], (CM, C), CM ** -0.5, 0.375, (), jnp.float32),
        "project_weight": noise(arg_keys[5], (C * C, P_SIZE), 0.5, 3.0, (), jnp.float32),
        "project_bias": noise(arg_keys[6], (P_SIZE,), 0.3, 1.75, (), jnp.float32),
        "pair_state": noise(arg_keys[7], (R, R, P_SIZE), 1.0, 6.0, ((0, 4), (1, 8)), jnp.float32),
        "pair_gain": jnp.clip(1.0 + 0.1 * jax.random.normal(arg_keys[8], (P_SIZE,), jnp.float32), 0.5, 1.5),
        "pair_bias": noise(arg_keys[9], (P_SIZE,), 0.3, 1.75, (), jnp.float32),
        "hidden_weight": noise(arg_keys[10], (P_SIZE, H), P_SIZE ** -0.5, 0.5, (), jnp.float32),
        "hidden_bias": noise(arg_keys[11], (H,), 0.3, 1.75, (), jnp.float32),
        "final_weight": noise(arg_keys[12], (H, P_SIZE), H ** -0.5, 0.25, (), jnp.float32),
        "final_bias": noise(arg_keys[13], (P_SIZE,), 0.3, 1.75, (), jnp.float32),
    }


def layer_norm(values, gain, offset):
    middle = lax.optimization_barrier(jnp.mean(values, axis=-1, keepdims=True))
    spread = lax.optimization_barrier(jnp.mean(jnp.square(values - middle), axis=-1, keepdims=True))
    return (values - middle) * lax.rsqrt(spread + 1e-05) * gain + offset

def reference(alignment, align_gain, align_bias, left_weight, right_weight, project_weight, project_bias, pair_state, pair_gain, pair_bias, hidden_weight, hidden_bias, final_weight, final_bias):
    highest = lax.Precision.HIGHEST
    normed = layer_norm(alignment, align_gain, align_bias).reshape(S * R, CM)
    left = jnp.dot(normed, left_weight, precision=highest, preferred_element_type=jnp.float32).reshape(S, R * C)
    right = jnp.dot(normed, right_weight, precision=highest, preferred_element_type=jnp.float32).reshape(S, R * C)
    block_rows = 16

    def one_block(index):
        piece = lax.dynamic_slice_in_dim(left, (index * block_rows * C).astype(jnp.int32), block_rows * C, 1)
        product = lax.dot_general(piece, right, (((0,), (0,)), ((), ())), precision=highest, preferred_element_type=jnp.float32) / S
        product = product.reshape(block_rows, C, R, C).transpose(0, 2, 1, 3).reshape(block_rows * R, C * C)
        return jnp.dot(product, project_weight, precision=highest, preferred_element_type=jnp.float32)
    update = lax.map(one_block, jnp.arange(R // block_rows, dtype=jnp.int32)).reshape(R, R, P_SIZE)
    updated = pair_state + update + project_bias
    flat = layer_norm(updated, pair_gain, pair_bias).reshape(R * R, P_SIZE)
    hidden = jax.nn.relu(jnp.dot(flat, hidden_weight, precision=highest, preferred_element_type=jnp.float32) + hidden_bias)
    output = jnp.dot(hidden, final_weight, precision=highest, preferred_element_type=jnp.float32) + final_bias
    return updated + output.reshape(R, R, P_SIZE)
```

```python
import functools

import jax
import jax.numpy as jnp
from jax import lax
from jax.experimental import pallas as pl
from jax.experimental.pallas import tpu as pltpu
from jax.sharding import PartitionSpec as P


LANES = 128
EPS = 1e-05
F32 = jnp.float32
BF16 = jnp.bfloat16


def split(values):
    high = values.astype(BF16)
    low = (values - high.astype(F32)).astype(BF16)
    return high, low


def dot(a, b):
    return jnp.dot(a, b, preferred_element_type=F32)


def norm(values, gain, offset):
    middle = jnp.mean(values, axis=-1, keepdims=True)
    centred = values - middle
    spread = jnp.mean(jnp.square(centred), axis=-1, keepdims=True)
    return centred * lax.rsqrt(spread + EPS) * gain + offset


def project_kernel(seqs, residues, width, chunks, x_ref, gain_ref, bias_ref, lw_ref, rw_ref, *refs):
    left_refs, right_ref = refs[:chunks], refs[chunks]
    w_high, w_low, y_ref, high_ref, low_ref = refs[chunks + 1 :]
    channels = x_ref.shape[1]
    per = LANES // width
    groups = residues // per

    @pl.when(pl.program_id(0) == 0)
    def _():
        for at, ref in enumerate((lw_ref, rw_ref)):
            weight = jnp.concatenate([ref[...], jnp.zeros((channels, LANES - width), F32)], axis=1)
            for e in range(per):
                placed = pltpu.roll(weight, e * width, 1) if e else weight
                high, low = split(placed)
                w_high[e * channels : (e + 1) * channels, at * LANES : (at + 1) * LANES] = high
                w_low[e * channels : (e + 1) * channels, at * LANES : (at + 1) * LANES] = low

    normed = norm(x_ref[...], gain_ref[...], bias_ref[...])
    for part in range(channels // LANES):
        y_ref[part] = normed[:, part * LANES : (part + 1) * LANES]
    for e in range(per):
        for g in range(groups):
            for part in range(channels // LANES):
                high, low = split(y_ref[part, pl.ds(g * per + e, seqs, stride=residues), :])
                first = e * channels + part * LANES
                high_ref[g * seqs : (g + 1) * seqs, first : first + LANES] = high
                low_ref[g * seqs : (g + 1) * seqs, first : first + LANES] = low
    both = dot(high_ref[...], w_high[...]) + dot(low_ref[...], w_high[...]) + dot(high_ref[...], w_low[...])
    share = groups // chunks
    for g in range(groups):
        rows = both[g * seqs : (g + 1) * seqs]
        at = g % share
        left_refs[g // share][:, at * LANES : (at + 1) * LANES] = rows[:, :LANES]
        right_ref[:, g * LANES : (g + 1) * LANES] = rows[:, LANES:]


def project(alignment, gain, bias, left_weight, right_weight, chunks):
    seq_local, residues, channels = alignment.shape
    width = left_weight.shape[1]
    steps = 2
    seqs = seq_local // steps
    per = LANES // width
    groups = residues // per
    span = residues * width
    whole = lambda shape: pl.BlockSpec(shape, lambda s: (0,) * len(shape))
    outs = [jax.ShapeDtypeStruct((seq_local, span // chunks), F32)] * chunks + [
        jax.ShapeDtypeStruct((seq_local, span), F32)
    ]
    return pl.pallas_call(
        functools.partial(project_kernel, seqs, residues, width, chunks),
        out_shape=outs,
        grid=(steps,),
        in_specs=[
            pl.BlockSpec((seqs * residues, channels), lambda s: (s, 0)),
            whole((1, channels)),
            whole((1, channels)),
            whole((channels, width)),
            whole((channels, width)),
        ],
        out_specs=[pl.BlockSpec((seqs, o.shape[1]), lambda s: (s, 0)) for o in outs],
        scratch_shapes=[
            pltpu.VMEM((per * channels, 2 * LANES), BF16),
            pltpu.VMEM((per * channels, 2 * LANES), BF16),
            pltpu.VMEM((channels // LANES, seqs * residues, LANES), F32),
            pltpu.VMEM((groups * seqs, per * channels), BF16),
            pltpu.VMEM((groups * seqs, per * channels), BF16),
        ],
        cost_estimate=pl.CostEstimate(flops=6 * 10**9, bytes_accessed=4 * 10**6, transcendentals=0),
        name="project",
    )(
        alignment.reshape(seq_local * residues, channels),
        gain.reshape(1, channels),
        bias.reshape(1, channels),
        left_weight,
        right_weight,
    )


def weights_kernel(width, wp_ref, wh_ref, wf_ref, wp_out, wh_out, wf_out):
    pair = wp_ref.shape[1]
    for d in range(width):
        high, low = split(wp_ref[pl.ds(d, width, stride=width), :])
        wp_out[d * width : (d + 1) * width, :pair] = high
        wp_out[d * width : (d + 1) * width, pair:] = low
    high, low = split(wh_ref[...])
    wh_out[:pair] = high
    wh_out[pair : 2 * pair] = high
    wh_out[2 * pair :] = low
    high, low = split(wf_ref[...])
    wf_out[:, :pair] = high
    wf_out[:, pair:] = low


def prepare_weights(project_weight, hidden_weight, final_weight, width):
    pair, hidden = hidden_weight.shape
    return pl.pallas_call(
        functools.partial(weights_kernel, width),
        out_shape=[
            jax.ShapeDtypeStruct((width * width, 2 * pair), BF16),
            jax.ShapeDtypeStruct((3 * pair, hidden), BF16),
            jax.ShapeDtypeStruct((hidden, 2 * pair), BF16),
        ],
        cost_estimate=pl.CostEstimate(flops=10**9, bytes_accessed=2 * 10**6, transcendentals=0),
        name="weights",
    )(project_weight, hidden_weight, final_weight)


def turn_kernel(residues, width, scale, *refs):
    parts, out_ref, turned = refs[:-2], refs[-2], refs[-1]
    seqs = parts[0].shape[0]
    total = seqs * len(parts)
    whole = jnp.concatenate([p[...] for p in parts], axis=0) * scale
    for part in range(total // LANES):
        turned[part] = whole[part * LANES : (part + 1) * LANES].T
    for d in range(width):
        rows = slice(d * residues, (d + 1) * residues)
        for part in range(total // LANES):
            high, low = split(turned[part, pl.ds(d, residues, stride=width), :])
            for at, value in ((0, high), (total, low), (2 * total, high)):
                first = at + part * LANES
                out_ref[rows, first : first + LANES] = value


def turn(parts, residues, width):
    seqs, span = parts[0].shape
    total = seqs * len(parts)
    return pl.pallas_call(
        functools.partial(turn_kernel, residues, width, 1.0 / total),
        out_shape=jax.ShapeDtypeStruct((span, 3 * total), BF16),
        scratch_shapes=[pltpu.VMEM((total // LANES, span, LANES), F32)],
        cost_estimate=pl.CostEstimate(flops=2 * 10**9, bytes_accessed=3 * 10**6, transcendentals=0),
        name="turn",
    )(*parts)


def route_kernel(slots, t_ref, *refs):
    ins, outs = refs[:-slots], refs[-slots:]
    for t in range(slots):

        @pl.when(t_ref[0] == t)
        def _():
            for m in range(slots):
                at = m ^ t
                value = ins[at][...]
                if at == slots - 1:
                    for extra in ins[slots:]:
                        value = value + extra[...]
                outs[m][...] = value


def route(t, slots, ins):
    spec = pl.BlockSpec(memory_space=pltpu.VMEM)
    return pl.pallas_call(
        functools.partial(route_kernel, slots),
        out_shape=[jax.ShapeDtypeStruct(ins[0].shape, F32)] * slots,
        in_specs=[pl.BlockSpec(memory_space=pltpu.SMEM)] + [spec] * len(ins),
        out_specs=[spec] * slots,
        cost_estimate=pl.CostEstimate(flops=10**6, bytes_accessed=2 * 10**6, transcendentals=0),
        name="route",
    )(t, *ins)


def pair_kernel(parts, tile, width, at_ref, *refs):
    l_refs = refs[:parts]
    rt_ref, wp_ref, wh_ref, wf_ref, pb_ref, pg_ref, po_ref, hb_ref, fb_ref, ps_ref = refs[parts : parts + 10]
    out_ref, high_ref, low_ref = refs[-3:]
    residues, pair = ps_ref.shape[1:]
    per = LANES // width
    left = jnp.concatenate([l[...] for l in l_refs], axis=0)
    high, low = split(left)
    left = jnp.concatenate([high, high, low], axis=0)
    lane = lax.broadcasted_iota(jnp.int32, (residues, LANES), 1) // width
    odd, upper = lane % 2 == 1, lane >= 2
    block = 2 * per
    for first in range(0, width, block):
        outer = dot(rt_ref[first * residues : (first + block) * residues, :], left)
        for d0 in range(0, block, per):
            for g in range(tile // per):
                u = []
                for d in range(per):
                    rows = (d0 + d) * residues
                    v = outer[rows : rows + residues, g * LANES : (g + 1) * LANES]
                    u.append(pltpu.roll(v, d * width, 1) if d else v)
                x = [jnp.where(odd, u[(n + 1) % per], u[n]) for n in range(per)]
                for i in range(per):
                    n = -i % per
                    y = jnp.where(upper, x[(n + 2) % per], x[n])
                    y = pltpu.roll(y, (per - i) * width, 1) if i else y
                    high, low = split(y)
                    rows = slice((g * per + i) * residues, (g * per + i + 1) * residues)
                    lanes = slice((first + d0) * width, (first + d0 + per) * width)
                    high_ref[rows, lanes] = high
                    low_ref[rows, lanes] = low
    both = dot(high_ref[...], wp_ref[...])
    update = both[:, :pair] + both[:, pair:] + dot(low_ref[...], wp_ref[:, :pair])
    updated = ps_ref[...].reshape(tile * residues, pair) + update + pb_ref[...]
    high, low = split(norm(updated, pg_ref[...], po_ref[...]))
    hidden = jnp.maximum(dot(jnp.concatenate([high, low, high], axis=1), wh_ref[...]) + hb_ref[...], 0.0)
    high, low = split(hidden)
    both = dot(high, wf_ref[...])
    output = both[:, :pair] + both[:, pair:] + dot(low, wf_ref[:, :pair]) + fb_ref[...]
    out_ref[...] = (updated + output).reshape(tile, residues, pair)


def pair_update(at, lefts, rt, weights, vectors, pair_state, out, width):
    tile = 8
    wp, wh, wf = weights
    seqs, span = lefts[0].shape
    steps = span // (tile * width)
    residues, pair = pair_state.shape[1:]
    whole = lambda a: pl.BlockSpec(a.shape, lambda s, at: (0,) * a.ndim, pipeline_mode=pl.Buffered(1))
    rows = pl.BlockSpec((tile, residues, pair), lambda s, at: (at[0] + s, 0, 0))
    operands = [*lefts, rt, wp, wh, wf, *vectors, pair_state]
    specs = [pl.BlockSpec((seqs, tile * width), lambda s, at: (0, s)) for _ in lefts]
    specs += [whole(a) for a in operands[len(lefts) : -1]] + [rows]
    aliases = {}
    if out is not None:
        aliases = {len(operands) + 1: 0}
        operands.append(out)
        specs.append(pl.BlockSpec(memory_space=pl.ANY))
    return pl.pallas_call(
        functools.partial(pair_kernel, len(lefts), tile, width),
        out_shape=jax.ShapeDtypeStruct(pair_state.shape, F32),
        grid_spec=pltpu.PrefetchScalarGridSpec(
            num_scalar_prefetch=1,
            grid=(steps,),
            in_specs=specs,
            out_specs=rows,
            scratch_shapes=[
                pltpu.VMEM((tile * residues, width * width), BF16),
                pltpu.VMEM((tile * residues, width * width), BF16),
            ],
        ),
        input_output_aliases=aliases,
        cost_estimate=pl.CostEstimate(flops=steps * 10**9, bytes_accessed=4 * 10**6, transcendentals=0),
        name="pair",
    )(at, *operands)


def on_device(
    alignment,
    align_gain,
    align_bias,
    left_weight,
    right_weight,
    project_weight,
    project_bias,
    pair_state,
    pair_gain,
    pair_bias,
    hidden_weight,
    hidden_bias,
    final_weight,
    final_bias,
):
    chunks = 1
    tile = 8
    seq_local, residues, channels = alignment.shape
    width = left_weight.shape[1]
    rows = lax.axis_size("row")
    cols = lax.axis_size("col")
    fold = cols // rows
    row = lax.axis_index("row")
    col = lax.axis_index("col")
    group, member = col // fold, col % fold

    def along_groups(value, pairs):
        return lax.ppermute(value, "col", [(a * fold + k, b * fold + k) for a, b in pairs for k in range(fold)])

    def along_rows(value, m):
        return lax.ppermute(value, "row", [(a, a ^ m) for a in range(rows)])

    def along_members(value, n):
        return lax.ppermute(value, "col", [(a, a ^ n) for a in range(cols)])

    *lefts, right = project(alignment, align_gain, align_bias, left_weight, right_weight, chunks)
    where = jnp.reshape(jnp.bitwise_xor(group, row).astype(jnp.int32), (1,))

    def spread(left):
        if rows != 4:
            return [left] + [along_groups(left, [(a, a ^ m) for a in range(rows)]) for m in range(1, rows)]
        two = along_groups(left, [(a, a ^ 2) for a in range(4)])
        one = along_groups(left, [(a, a ^ 1) for a in range(4)])
        three = along_groups(left, [(1, 2), (2, 1)])
        relayed = along_groups(two, [(1, 0), (2, 3)])
        return [left, one, two, three, relayed]

    slots = [spread(left) for left in lefts]
    rights = [right] + [along_rows(right, m) for m in range(1, rows)]
    weights = prepare_weights(project_weight, hidden_weight, final_weight, width)
    rt = turn(rights, residues, width)
    vectors = [v.reshape(1, -1) for v in (project_bias, pair_gain, pair_bias, hidden_bias, final_bias)]

    out = None
    for chunk in range(chunks):
        routed = route(where, rows, slots[chunk])
        mine = [routed[0]] + [along_rows(routed[m], m) for m in range(1, rows)]
        packed = jnp.concatenate(mine, axis=0)
        for n in range(fold):
            block = [packed if n == 0 else along_members(packed, n)]
            tiles = residues // tile
            at = jnp.bitwise_xor(member, n) * tiles + chunk * (tiles // chunks)
            at = jnp.reshape(at.astype(jnp.int32), (1,))
            out = pair_update(at, block, rt, weights, vectors, pair_state, out, width)
    return out


def solution(mesh):
    placed = (
        P("row", "col", None),
        P(),
        P(),
        P(),
        P(),
        P(),
        P(),
        P("row", "col", None),
        P(),
        P(),
        P(),
        P(),
        P(),
        P(),
    )
    return jax.shard_map(
        on_device, mesh=mesh, in_specs=placed, out_specs=P("row", "col", None), check_vma=False
    )
```

```python
import functools

import jax
import jax.numpy as jnp
from jax import lax
from jax.experimental import pallas as pl
from jax.experimental.pallas import tpu as pltpu
from jax.sharding import PartitionSpec as P


LANES = 128
VMEM = 16 * 2**20
EPS = 1e-05
F32 = jnp.float32
BF16 = jnp.bfloat16


def split(values):
    high = values.astype(BF16)
    low = (values - high.astype(F32)).astype(BF16)
    return high, low


def dot(a, b):
    return jnp.dot(a, b, preferred_element_type=F32)


def norm(values, gain, offset):
    middle = jnp.mean(values, axis=-1, keepdims=True)
    centred = values - middle
    spread = jnp.mean(jnp.square(centred), axis=-1, keepdims=True)
    return centred * lax.rsqrt(spread + EPS) * gain + offset


def project_kernel(seqs, residues, width, chunks, x_hbm, gain_hbm, bias_hbm, lw_hbm, rw_hbm, *refs):
    left_refs, right_ref, place_ref = refs[:chunks], refs[chunks], refs[chunks + 1]
    x_ref, gain_ref, bias_ref, lw_ref, rw_ref, sems, w_high, w_low, y_ref, high_ref, low_ref = refs[chunks + 2 :]
    fold = lax.axis_size("col") // lax.axis_size("row")
    col = lax.axis_index("col")
    place_ref[0] = jnp.bitwise_xor(lax.div(col, fold), lax.axis_index("row")).astype(jnp.int32)
    place_ref[1] = lax.rem(col, fold).astype(jnp.int32)
    channels = x_ref.shape[1]
    per = LANES // width
    groups = residues // per
    block = seqs * residues
    steps = x_ref.shape[0] // block

    small = ((lw_hbm, lw_ref), (rw_hbm, rw_ref), (gain_hbm, gain_ref), (bias_hbm, bias_ref))
    copies = [pltpu.make_async_copy(a, b, sems.at[n]) for n, (a, b) in enumerate(small)]
    for step in range(steps):
        rows = pl.ds(step * block, block)
        copies.append(pltpu.make_async_copy(x_hbm.at[rows], x_ref.at[rows], sems.at[len(small) + step]))
    for copy in copies:
        copy.start()
    for copy in copies[: len(small)]:
        copy.wait()
    for at, ref in enumerate((lw_ref, rw_ref)):
        for e in range(per):
            zeros = [jnp.zeros((n * width, channels), F32) for n in (e, per - 1 - e)]
            placed = jnp.concatenate([z for z in (zeros[0], ref[...], zeros[1]) if z.shape[0]], axis=0)
            high, low = split(placed.T)
            w_high[e * channels : (e + 1) * channels, at * LANES : (at + 1) * LANES] = high
            w_low[e * channels : (e + 1) * channels, at * LANES : (at + 1) * LANES] = low

    for step in range(steps):
        copies[len(small) + step].wait()
        normed = norm(x_ref[step * block : (step + 1) * block, :], gain_ref[...], bias_ref[...])
        for part in range(channels // LANES):
            y_ref[step, part] = normed[:, part * LANES : (part + 1) * LANES]
        for e in range(per):
            for g in range(groups):
                for part in range(channels // LANES):
                    high, low = split(y_ref[step, part, pl.ds(g * per + e, seqs, stride=residues), :])
                    first = e * channels + part * LANES
                    high_ref[step, g * seqs : (g + 1) * seqs, first : first + LANES] = high
                    low_ref[step, g * seqs : (g + 1) * seqs, first : first + LANES] = low
        high, low = high_ref[step], low_ref[step]
        both = dot(high, w_high[...]) + dot(low, w_high[...]) + dot(high, w_low[...])
        share = groups // chunks
        for g in range(groups):
            rows = both[g * seqs : (g + 1) * seqs]
            to = slice(step * seqs, (step + 1) * seqs)
            at = g % share
            left_refs[g // share][to, at * LANES : (at + 1) * LANES] = rows[:, :LANES]
            right_ref[to, g * LANES : (g + 1) * LANES] = rows[:, LANES:]


def project(alignment, gain, bias, left_weight, right_weight, chunks):
    seq_local, residues, channels = alignment.shape
    width = left_weight.shape[1]
    steps = 4
    seqs = seq_local // steps
    per = LANES // width
    groups = residues // per
    span = residues * width
    outs = [jax.ShapeDtypeStruct((seq_local, span // chunks), F32)] * chunks + [
        jax.ShapeDtypeStruct((seq_local, span), F32),
        jax.ShapeDtypeStruct((2,), jnp.int32),
    ]
    return pl.pallas_call(
        functools.partial(project_kernel, seqs, residues, width, chunks),
        out_shape=outs,
        in_specs=[pl.BlockSpec(memory_space=pltpu.HBM)] * 5,
        out_specs=[pl.BlockSpec(memory_space=pltpu.VMEM)] * (len(outs) - 1) + [pl.BlockSpec(memory_space=pltpu.SMEM)],
        scratch_shapes=[
            pltpu.VMEM((seq_local * residues, channels), F32),
            pltpu.VMEM((1, channels), F32),
            pltpu.VMEM((1, channels), F32),
            pltpu.VMEM((width, channels), F32),
            pltpu.VMEM((width, channels), F32),
            pltpu.SemaphoreType.DMA((4 + steps,)),
            pltpu.VMEM((per * channels, 2 * LANES), BF16),
            pltpu.VMEM((per * channels, 2 * LANES), BF16),
            pltpu.VMEM((steps, channels // LANES, seqs * residues, LANES), F32),
            pltpu.VMEM((steps, groups * seqs, per * channels), BF16),
            pltpu.VMEM((steps, groups * seqs, per * channels), BF16),
        ],
        cost_estimate=pl.CostEstimate(flops=6 * 10**9, bytes_accessed=4 * 10**6, transcendentals=0),
        compiler_params=pltpu.CompilerParams(vmem_limit_bytes=VMEM),
        name="project",
    )(
        *(
            pltpu.with_memory_space_constraint(a, pltpu.HBM)
            for a in (
                alignment.reshape(seq_local * residues, channels),
                gain.reshape(1, channels),
                bias.reshape(1, channels),
                left_weight.T,
                right_weight.T,
            )
        )
    )


def weights_kernel(width, wp_ref, wh_ref, wf_ref, wp_out, wh_out, wf_out):
    pair = wp_ref.shape[1]
    for d in range(width):
        high, low = split(wp_ref[pl.ds(d, width, stride=width), :])
        wp_out[d * width : (d + 1) * width, :pair] = high
        wp_out[d * width : (d + 1) * width, pair:] = low
    high, low = split(wh_ref[...])
    wh_out[:pair] = high
    wh_out[pair : 2 * pair] = high
    wh_out[2 * pair :] = low
    high, low = split(wf_ref[...])
    wf_out[:, :pair] = high
    wf_out[:, pair:] = low


def prepare_weights(project_weight, hidden_weight, final_weight, width):
    pair, hidden = hidden_weight.shape
    return pl.pallas_call(
        functools.partial(weights_kernel, width),
        out_shape=[
            jax.ShapeDtypeStruct((width * width, 2 * pair), BF16),
            jax.ShapeDtypeStruct((3 * pair, hidden), BF16),
            jax.ShapeDtypeStruct((hidden, 2 * pair), BF16),
        ],
        cost_estimate=pl.CostEstimate(flops=10**9, bytes_accessed=2 * 10**6, transcendentals=0),
        compiler_params=pltpu.CompilerParams(vmem_limit_bytes=VMEM),
        name="weights",
    )(project_weight, hidden_weight, final_weight)


def turn_kernel(residues, width, scale, *refs):
    parts, out_ref, turned = refs[:-2], refs[-2], refs[-1]
    seqs = parts[0].shape[0]
    total = seqs * len(parts)
    whole = jnp.concatenate([p[...] for p in parts], axis=0) * scale
    for part in range(total // LANES):
        turned[part] = whole[part * LANES : (part + 1) * LANES].T
    for d in range(width):
        rows = slice(d * residues, (d + 1) * residues)
        for part in range(total // LANES):
            high, low = split(turned[part, pl.ds(d, residues, stride=width), :])
            for at, value in ((0, high), (total, low), (2 * total, high)):
                first = at + part * LANES
                out_ref[rows, first : first + LANES] = value


def turn(parts, residues, width):
    seqs, span = parts[0].shape
    total = seqs * len(parts)
    return pl.pallas_call(
        functools.partial(turn_kernel, residues, width, 1.0 / total),
        out_shape=jax.ShapeDtypeStruct((span, 3 * total), BF16),
        scratch_shapes=[pltpu.VMEM((total // LANES, span, LANES), F32)],
        cost_estimate=pl.CostEstimate(flops=2 * 10**9, bytes_accessed=3 * 10**6, transcendentals=0),
        compiler_params=pltpu.CompilerParams(vmem_limit_bytes=VMEM),
        name="turn",
    )(*parts)


def route_kernel(slots, t_ref, *refs):
    ins, outs = refs[:-slots], refs[-slots:]
    for t in range(slots):

        @pl.when(t_ref[0] == t)
        def _():
            for m in range(slots):
                at = m ^ t
                value = ins[at][...]
                if at == slots - 1:
                    for extra in ins[slots:]:
                        value = value + extra[...]
                outs[m][...] = value


def route(t, slots, ins):
    spec = pl.BlockSpec(memory_space=pltpu.VMEM)
    return pl.pallas_call(
        functools.partial(route_kernel, slots),
        out_shape=[jax.ShapeDtypeStruct(ins[0].shape, F32)] * slots,
        in_specs=[pl.BlockSpec(memory_space=pltpu.SMEM)] + [spec] * len(ins),
        out_specs=[spec] * slots,
        cost_estimate=pl.CostEstimate(flops=10**6, bytes_accessed=2 * 10**6, transcendentals=0),
        compiler_params=pltpu.CompilerParams(vmem_limit_bytes=VMEM),
        name="route",
    )(t, *ins)


def pack_kernel(*refs):
    rows = refs[0].shape[0]
    for n, ref in enumerate(refs[:-1]):
        refs[-1][n * rows : (n + 1) * rows, :] = ref[...]


def pack(parts):
    rows, span = parts[0].shape
    return pl.pallas_call(
        pack_kernel,
        out_shape=jax.ShapeDtypeStruct((rows * len(parts), span), F32),
        cost_estimate=pl.CostEstimate(flops=10**6, bytes_accessed=10**6, transcendentals=0),
        compiler_params=pltpu.CompilerParams(vmem_limit_bytes=VMEM),
        name="pack",
    )(*parts)


def pair_kernel(parts, steps, tile, width, at_ref, *refs):
    l_refs = refs[:parts]
    rt_ref, wp_ref, wh_ref, wf_ref, pb_ref, pg_ref, po_ref, hb_ref, fb_ref, ps_ref = refs[parts : parts + 10]
    out_ref, high_ref, low_ref = refs[-3:]
    residues, pair = ps_ref.shape[1:]
    per = LANES // width
    left = l_refs[0][...]
    for n in range(1, parts):
        left = jnp.where(pl.program_id(0) >= n * steps, l_refs[n][...], left)
    high, low = split(left)
    left = jnp.concatenate([high, high, low], axis=0)
    lane = lax.broadcasted_iota(jnp.int32, (residues, LANES), 1) // width
    odd, upper = lane % 2 == 1, lane >= 2
    block = 2 * per
    for first in range(0, width, block):
        outer = dot(rt_ref[first * residues : (first + block) * residues, :], left)
        for d0 in range(0, block, per):
            for g in range(tile // per):
                u = []
                for d in range(per):
                    rows = (d0 + d) * residues
                    v = outer[rows : rows + residues, g * LANES : (g + 1) * LANES]
                    u.append(pltpu.roll(v, d * width, 1) if d else v)
                x = [jnp.where(odd, u[(n + 1) % per], u[n]) for n in range(per)]
                for i in range(per):
                    n = -i % per
                    y = jnp.where(upper, x[(n + 2) % per], x[n])
                    y = pltpu.roll(y, (per - i) * width, 1) if i else y
                    high, low = split(y)
                    rows = slice((g * per + i) * residues, (g * per + i + 1) * residues)
                    lanes = slice((first + d0) * width, (first + d0 + per) * width)
                    high_ref[rows, lanes] = high
                    low_ref[rows, lanes] = low
    both = dot(high_ref[...], wp_ref[...])
    update = both[:, :pair] + both[:, pair:] + dot(low_ref[...], wp_ref[:, :pair])
    updated = ps_ref[...].reshape(tile * residues, pair) + update + pb_ref[...]
    high, low = split(norm(updated, pg_ref[...], po_ref[...]))
    hidden = jnp.maximum(dot(jnp.concatenate([high, low, high], axis=1), wh_ref[...]) + hb_ref[...], 0.0)
    high, low = split(hidden)
    both = dot(high, wf_ref[...])
    output = both[:, :pair] + both[:, pair:] + dot(low, wf_ref[:, :pair]) + fb_ref[...]
    out_ref[...] = (updated + output).reshape(tile, residues, pair)


def pair_update(place, members, chunk, lefts, rt, weights, vectors, pair_state, out, width):
    tile = 8
    wp, wh, wf = weights
    seqs, span = lefts[0].shape
    steps = span // (tile * width)
    residues, pair = pair_state.shape[1:]
    whole = lambda a: pl.BlockSpec(a.shape, lambda s, at: (0,) * a.ndim, pipeline_mode=pl.Buffered(1))
    tiles = residues // tile

    def tile_at(s, place):
        member = jnp.bitwise_xor(place[1], members[0])
        for n in range(1, len(members)):
            member = jnp.where(s >= n * steps, jnp.bitwise_xor(place[1], members[n]), member)
        return member * tiles + chunk * steps + lax.rem(s, steps), 0, 0

    rows = pl.BlockSpec((tile, residues, pair), tile_at)
    fixed = [pltpu.with_memory_space_constraint(a, pltpu.VMEM) for a in (rt, wp, wh, wf)]
    operands = [*lefts, *fixed, *vectors, pair_state]
    specs = [
        pl.BlockSpec((seqs, tile * width), lambda s, at, n=n: (0, jnp.clip(s - n * steps, 0, steps - 1)))
        for n in range(len(lefts))
    ]
    specs += [whole(a) for a in operands[len(lefts) : -1]] + [rows]
    aliases = {}
    if out is not None:
        aliases = {len(operands) + 1: 0}
        operands.append(out)
        specs.append(pl.BlockSpec(memory_space=pl.ANY))
    return pl.pallas_call(
        functools.partial(pair_kernel, len(lefts), steps, tile, width),
        out_shape=jax.ShapeDtypeStruct(pair_state.shape, F32),
        grid_spec=pltpu.PrefetchScalarGridSpec(
            num_scalar_prefetch=1,
            grid=(steps * len(lefts),),
            in_specs=specs,
            out_specs=rows,
            scratch_shapes=[
                pltpu.VMEM((tile * residues, width * width), BF16),
                pltpu.VMEM((tile * residues, width * width), BF16),
            ],
        ),
        input_output_aliases=aliases,
        cost_estimate=pl.CostEstimate(flops=steps * len(lefts) * 10**9, bytes_accessed=4 * 10**6, transcendentals=0),
        compiler_params=pltpu.CompilerParams(vmem_limit_bytes=VMEM),
        name="pair",
    )(place, *operands)


def on_device(
    alignment,
    align_gain,
    align_bias,
    left_weight,
    right_weight,
    project_weight,
    project_bias,
    pair_state,
    pair_gain,
    pair_bias,
    hidden_weight,
    hidden_bias,
    final_weight,
    final_bias,
):
    chunks = 2
    residues = alignment.shape[1]
    width = left_weight.shape[1]
    rows = lax.axis_size("row")
    cols = lax.axis_size("col")
    fold = cols // rows

    def along_groups(value, pairs):
        return lax.ppermute(value, "col", [(a * fold + k, b * fold + k) for a, b in pairs for k in range(fold)])

    def along_rows(value, m):
        return lax.ppermute(value, "row", [(a, a ^ m) for a in range(rows)])

    def along_members(value, n):
        return lax.ppermute(value, "col", [(a, a ^ n) for a in range(cols)])

    *lefts, right, place = project(alignment, align_gain, align_bias, left_weight, right_weight, chunks)

    def spread(left):
        if rows != 4:
            return [left] + [along_groups(left, [(a, a ^ m) for a in range(rows)]) for m in range(1, rows)]
        two = along_groups(left, [(a, a ^ 2) for a in range(4)])
        one = along_groups(left, [(a, a ^ 1) for a in range(4)])
        three = along_groups(left, [(1, 2), (2, 1)])
        relayed = along_groups(two, [(1, 0), (2, 3)])
        return [left, one, two, three, relayed]

    slots = [spread(left) for left in lefts]
    rights = [right] + [along_rows(right, m) for m in range(1, rows)]
    weights = prepare_weights(project_weight, hidden_weight, final_weight, width)
    rt = turn(rights, residues, width)
    vectors = [v.reshape(1, -1) for v in (project_bias, pair_gain, pair_bias, hidden_bias, final_bias)]

    out = None
    for chunk in range(chunks):
        routed = route(place, rows, slots[chunk])
        mine = [routed[0]] + [along_rows(routed[m], m) for m in range(1, rows)]
        packed = pack(mine)
        blocks = [packed] + [along_members(packed, n) for n in range(1, fold)]
        calls = [[n] for n in range(fold)] if chunk == chunks - 1 else [list(range(fold))]
        for members in calls:
            out = pair_update(
                place, members, chunk, [blocks[n] for n in members], rt, weights, vectors, pair_state, out, width
            )
    return out


def solution(mesh):
    placed = (
        P("row", "col", None),
        P(),
        P(),
        P(),
        P(),
        P(),
        P(),
        P("row", "col", None),
        P(),
        P(),
        P(),
        P(),
        P(),
        P(),
    )

    return jax.shard_map(on_device, mesh=mesh, in_specs=placed, out_specs=P("row", "col", None), check_vma=False)
```

```python
import functools

import jax
import jax.numpy as jnp
from jax import lax
from jax.experimental import pallas as pl
from jax.experimental.pallas import tpu as pltpu
from jax.sharding import PartitionSpec as P


LANES = 128
VMEM = 16 * 2**20
EPS = 1e-05
F32 = jnp.float32
BF16 = jnp.bfloat16


def split(values):
    high = values.astype(BF16)
    low = (values - high.astype(F32)).astype(BF16)
    return high, low


def dot(a, b):
    return jnp.dot(a, b, preferred_element_type=F32)


def norm(values, gain, offset):
    middle = jnp.mean(values, axis=-1, keepdims=True)
    centred = values - middle
    spread = jnp.mean(jnp.square(centred), axis=-1, keepdims=True)
    return centred * lax.rsqrt(spread + EPS) * gain + offset


def project_kernel(seqs, residues, width, chunks, x_hbm, gain_hbm, bias_hbm, lw_hbm, rw_hbm, *refs):
    left_refs, right_ref, place_ref = refs[:chunks], refs[chunks], refs[chunks + 1]
    x_ref, gain_ref, bias_ref, lw_ref, rw_ref, sems, w_ref, p_ref = refs[chunks + 2 :]
    fold = lax.axis_size("col") // lax.axis_size("row")
    col = lax.axis_index("col")
    place_ref[0] = jnp.bitwise_xor(lax.div(col, fold), lax.axis_index("row")).astype(jnp.int32)
    place_ref[1] = lax.rem(col, fold).astype(jnp.int32)
    channels = x_ref.shape[1]
    per = LANES // width
    groups = residues // per
    block = seqs * residues
    steps = x_ref.shape[0] // block

    small = ((lw_hbm, lw_ref), (rw_hbm, rw_ref), (gain_hbm, gain_ref), (bias_hbm, bias_ref))
    copies = [pltpu.make_async_copy(a, b, sems.at[n]) for n, (a, b) in enumerate(small)]
    for step in range(steps):
        rows = pl.ds(step * block, block)
        copies.append(pltpu.make_async_copy(x_hbm.at[rows], x_ref.at[rows], sems.at[len(small) + step]))
    for copy in copies:
        copy.start()
    for copy in copies[: len(small)]:
        copy.wait()
    plain = jnp.concatenate([lw_ref[...], rw_ref[...]], axis=0)
    high, low = split(jnp.concatenate([plain * gain_ref[...], plain], axis=0).T)
    w_ref[:, :LANES] = high
    w_ref[:, LANES:] = low

    def multiply(values):
        high, low = split(values)
        both = dot(high, w_ref[...])
        return both[:, :LANES] + both[:, LANES:] + dot(low, w_ref[:, :LANES])

    offset = multiply(jnp.broadcast_to(bias_ref[...], (8, channels)))
    offset = pltpu.roll(offset, LANES - 2 * width, 1)[:1]
    lane = lax.broadcasted_iota(jnp.int32, (seqs, LANES), 1) // width
    share = groups // chunks
    for step in range(steps):
        copies[len(small) + step].wait()
        x = x_ref[step * block : (step + 1) * block, :]
        centred = x - jnp.mean(x, axis=-1, keepdims=True)
        spread = jnp.mean(jnp.square(centred), axis=-1, keepdims=True)
        p_ref[step] = multiply(centred) * lax.rsqrt(spread + EPS) + offset
        to = slice(step * seqs, (step + 1) * seqs)
        for g in range(groups):
            rows = [p_ref[step, pl.ds(g * per + e, seqs, stride=residues), :] for e in range(per)]
            for side in range(2):
                value = None
                for e in range(per):
                    shift = (e - side) % per * width
                    placed = pltpu.roll(rows[e], shift, 1) if shift else rows[e]
                    value = placed if value is None else jnp.where(lane == e, placed, value)
                if side:
                    right_ref[to, g * LANES : (g + 1) * LANES] = value
                else:
                    at = g % share
                    left_refs[g // share][to, at * LANES : (at + 1) * LANES] = value


def project(alignment, gain, bias, left_weight, right_weight, chunks):
    seq_local, residues, channels = alignment.shape
    width = left_weight.shape[1]
    steps = 4
    seqs = seq_local // steps
    span = residues * width
    outs = [jax.ShapeDtypeStruct((seq_local, span // chunks), F32)] * chunks + [
        jax.ShapeDtypeStruct((seq_local, span), F32),
        jax.ShapeDtypeStruct((2,), jnp.int32),
    ]
    return pl.pallas_call(
        functools.partial(project_kernel, seqs, residues, width, chunks),
        out_shape=outs,
        in_specs=[pl.BlockSpec(memory_space=pltpu.HBM)] * 5,
        out_specs=[pl.BlockSpec(memory_space=pltpu.VMEM)] * (len(outs) - 1) + [pl.BlockSpec(memory_space=pltpu.SMEM)],
        scratch_shapes=[
            pltpu.VMEM((seq_local * residues, channels), F32),
            pltpu.VMEM((1, channels), F32),
            pltpu.VMEM((1, channels), F32),
            pltpu.VMEM((width, channels), F32),
            pltpu.VMEM((width, channels), F32),
            pltpu.SemaphoreType.DMA((4 + steps,)),
            pltpu.VMEM((channels, 2 * LANES), BF16),
            pltpu.VMEM((steps, seqs * residues, LANES), F32),
        ],
        cost_estimate=pl.CostEstimate(flops=6 * 10**9, bytes_accessed=4 * 10**6, transcendentals=0),
        compiler_params=pltpu.CompilerParams(vmem_limit_bytes=VMEM),
        name="project",
    )(
        *(
            pltpu.with_memory_space_constraint(a, pltpu.HBM)
            for a in (
                alignment.reshape(seq_local * residues, channels),
                gain.reshape(1, channels),
                bias.reshape(1, channels),
                left_weight.T,
                right_weight.T,
            )
        )
    )


def weights_kernel(width, wp_ref, wh_ref, wf_ref, wp_out, wh_out, wf_out):
    pair = wp_ref.shape[1]
    for d in range(width):
        high, low = split(wp_ref[pl.ds(d, width, stride=width), :])
        wp_out[d * width : (d + 1) * width, :pair] = high
        wp_out[d * width : (d + 1) * width, pair:] = low
    high, low = split(wh_ref[...])
    wh_out[:pair] = high
    wh_out[pair : 2 * pair] = high
    wh_out[2 * pair :] = low
    high, low = split(wf_ref[...])
    wf_out[:, :pair] = high
    wf_out[:, pair:] = low


def prepare_weights(project_weight, hidden_weight, final_weight, width):
    pair, hidden = hidden_weight.shape
    return pl.pallas_call(
        functools.partial(weights_kernel, width),
        out_shape=[
            jax.ShapeDtypeStruct((width * width, 2 * pair), BF16),
            jax.ShapeDtypeStruct((3 * pair, hidden), BF16),
            jax.ShapeDtypeStruct((hidden, 2 * pair), BF16),
        ],
        cost_estimate=pl.CostEstimate(flops=10**9, bytes_accessed=2 * 10**6, transcendentals=0),
        compiler_params=pltpu.CompilerParams(vmem_limit_bytes=VMEM),
        name="weights",
    )(project_weight, hidden_weight, final_weight)


def turn_kernel(residues, width, scale, *refs):
    parts, out_ref, turned = refs[:-2], refs[-2], refs[-1]
    seqs = parts[0].shape[0]
    total = seqs * len(parts)
    whole = jnp.concatenate([p[...] for p in parts], axis=0) * scale
    for part in range(total // LANES):
        turned[part] = whole[part * LANES : (part + 1) * LANES].T
    for d in range(width):
        rows = slice(d * residues, (d + 1) * residues)
        for part in range(total // LANES):
            high, low = split(turned[part, pl.ds(d, residues, stride=width), :])
            for at, value in ((0, high), (total, low), (2 * total, high)):
                first = at + part * LANES
                out_ref[rows, first : first + LANES] = value


def turn(parts, residues, width):
    seqs, span = parts[0].shape
    total = seqs * len(parts)
    return pl.pallas_call(
        functools.partial(turn_kernel, residues, width, 1.0 / total),
        out_shape=jax.ShapeDtypeStruct((span, 3 * total), BF16),
        scratch_shapes=[pltpu.VMEM((total // LANES, span, LANES), F32)],
        cost_estimate=pl.CostEstimate(flops=2 * 10**9, bytes_accessed=3 * 10**6, transcendentals=0),
        compiler_params=pltpu.CompilerParams(vmem_limit_bytes=VMEM),
        name="turn",
    )(*parts)


def route_kernel(slots, t_ref, *refs):
    ins, outs = refs[:-slots], refs[-slots:]
    for t in range(slots):

        @pl.when(t_ref[0] == t)
        def _():
            for m in range(slots):
                at = m ^ t
                value = ins[at][...]
                if at == slots - 1:
                    for extra in ins[slots:]:
                        value = value + extra[...]
                outs[m][...] = value


def route(t, slots, ins):
    spec = pl.BlockSpec(memory_space=pltpu.VMEM)
    return pl.pallas_call(
        functools.partial(route_kernel, slots),
        out_shape=[jax.ShapeDtypeStruct(ins[0].shape, F32)] * slots,
        in_specs=[pl.BlockSpec(memory_space=pltpu.SMEM)] + [spec] * len(ins),
        out_specs=[spec] * slots,
        cost_estimate=pl.CostEstimate(flops=10**6, bytes_accessed=2 * 10**6, transcendentals=0),
        compiler_params=pltpu.CompilerParams(vmem_limit_bytes=VMEM),
        name="route",
    )(t, *ins)


def pack_kernel(*refs):
    rows = refs[0].shape[0]
    for n, ref in enumerate(refs[:-1]):
        refs[-1][n * rows : (n + 1) * rows, :] = ref[...]


def pack(parts):
    rows, span = parts[0].shape
    return pl.pallas_call(
        pack_kernel,
        out_shape=jax.ShapeDtypeStruct((rows * len(parts), span), F32),
        cost_estimate=pl.CostEstimate(flops=10**6, bytes_accessed=10**6, transcendentals=0),
        compiler_params=pltpu.CompilerParams(vmem_limit_bytes=VMEM),
        name="pack",
    )(*parts)


def pair_kernel(parts, steps, tile, width, at_ref, *refs):
    l_refs = refs[:parts]
    rt_ref, wp_ref, wh_ref, wf_ref, pb_ref, pg_ref, po_ref, hb_ref, fb_ref, ps_ref = refs[parts : parts + 10]
    out_ref, high_ref, low_ref = refs[-3:]
    residues, pair = ps_ref.shape[1:]
    per = LANES // width
    left = l_refs[0][...]
    for n in range(1, parts):
        left = jnp.where(pl.program_id(0) >= n * steps, l_refs[n][...], left)
    high, low = split(left)
    left = jnp.concatenate([high, high, low], axis=0)
    lane = lax.broadcasted_iota(jnp.int32, (residues, LANES), 1) // width
    odd, upper = lane % 2 == 1, lane >= 2
    block = 2 * per
    for first in range(0, width, block):
        outer = dot(rt_ref[first * residues : (first + block) * residues, :], left)
        for d0 in range(0, block, per):
            for g in range(tile // per):
                u = []
                for d in range(per):
                    rows = (d0 + d) * residues
                    v = outer[rows : rows + residues, g * LANES : (g + 1) * LANES]
                    u.append(pltpu.roll(v, d * width, 1) if d else v)
                x = [jnp.where(odd, u[(n + 1) % per], u[n]) for n in range(per)]
                for i in range(per):
                    n = -i % per
                    y = jnp.where(upper, x[(n + 2) % per], x[n])
                    y = pltpu.roll(y, (per - i) * width, 1) if i else y
                    high, low = split(y)
                    rows = slice((g * per + i) * residues, (g * per + i + 1) * residues)
                    lanes = slice((first + d0) * width, (first + d0 + per) * width)
                    high_ref[rows, lanes] = high
                    low_ref[rows, lanes] = low
    both = dot(high_ref[...], wp_ref[...])
    update = both[:, :pair] + both[:, pair:] + dot(low_ref[...], wp_ref[:, :pair])
    updated = ps_ref[...].reshape(tile * residues, pair) + update + pb_ref[...]
    high, low = split(norm(updated, pg_ref[...], po_ref[...]))
    hidden = jnp.maximum(dot(jnp.concatenate([high, low, high], axis=1), wh_ref[...]) + hb_ref[...], 0.0)
    high, low = split(hidden)
    both = dot(high, wf_ref[...])
    output = both[:, :pair] + both[:, pair:] + dot(low, wf_ref[:, :pair]) + fb_ref[...]
    out_ref[...] = (updated + output).reshape(tile, residues, pair)


def pair_update(place, members, chunk, lefts, rt, weights, vectors, pair_state, out, width):
    tile = 16
    wp, wh, wf = weights
    seqs, span = lefts[0].shape
    steps = span // (tile * width)
    residues, pair = pair_state.shape[1:]
    whole = lambda a: pl.BlockSpec(a.shape, lambda s, at: (0,) * a.ndim, pipeline_mode=pl.Buffered(1))
    tiles = residues // tile

    def tile_at(s, place):
        member = jnp.bitwise_xor(place[1], members[0])
        for n in range(1, len(members)):
            member = jnp.where(s >= n * steps, jnp.bitwise_xor(place[1], members[n]), member)
        return member * tiles + chunk * steps + lax.rem(s, steps), 0, 0

    rows = pl.BlockSpec((tile, residues, pair), tile_at)
    fixed = [pltpu.with_memory_space_constraint(a, pltpu.VMEM) for a in (rt, wp, wh, wf)]
    operands = [*lefts, *fixed, *vectors, pair_state]
    specs = [
        pl.BlockSpec((seqs, tile * width), lambda s, at, n=n: (0, jnp.clip(s - n * steps, 0, steps - 1)))
        for n in range(len(lefts))
    ]
    specs += [whole(a) for a in operands[len(lefts) : -1]] + [rows]
    aliases = {}
    if out is not None:
        aliases = {len(operands) + 1: 0}
        operands.append(out)
        specs.append(pl.BlockSpec(memory_space=pl.ANY))
    return pl.pallas_call(
        functools.partial(pair_kernel, len(lefts), steps, tile, width),
        out_shape=jax.ShapeDtypeStruct(pair_state.shape, F32),
        grid_spec=pltpu.PrefetchScalarGridSpec(
            num_scalar_prefetch=1,
            grid=(steps * len(lefts),),
            in_specs=specs,
            out_specs=rows,
            scratch_shapes=[
                pltpu.VMEM((tile * residues, width * width), BF16),
                pltpu.VMEM((tile * residues, width * width), BF16),
            ],
        ),
        input_output_aliases=aliases,
        cost_estimate=pl.CostEstimate(flops=steps * len(lefts) * 10**9, bytes_accessed=4 * 10**6, transcendentals=0),
        compiler_params=pltpu.CompilerParams(vmem_limit_bytes=VMEM),
        name="pair",
    )(place, *operands)


def on_device(
    alignment,
    align_gain,
    align_bias,
    left_weight,
    right_weight,
    project_weight,
    project_bias,
    pair_state,
    pair_gain,
    pair_bias,
    hidden_weight,
    hidden_bias,
    final_weight,
    final_bias,
):
    chunks = 2
    residues = alignment.shape[1]
    width = left_weight.shape[1]
    rows = lax.axis_size("row")
    cols = lax.axis_size("col")
    fold = cols // rows

    def along_groups(value, pairs):
        return lax.ppermute(value, "col", [(a * fold + k, b * fold + k) for a, b in pairs for k in range(fold)])

    def along_rows(value, m):
        return lax.ppermute(value, "row", [(a, a ^ m) for a in range(rows)])

    def along_members(value, n):
        return lax.ppermute(value, "col", [(a, a ^ n) for a in range(cols)])

    *lefts, right, place = project(alignment, align_gain, align_bias, left_weight, right_weight, chunks)

    def spread(left):
        if rows != 4:
            return [left] + [along_groups(left, [(a, a ^ m) for a in range(rows)]) for m in range(1, rows)]
        two = along_groups(left, [(a, a ^ 2) for a in range(4)])
        one = along_groups(left, [(a, a ^ 1) for a in range(4)])
        three = along_groups(left, [(1, 2), (2, 1)])
        relayed = along_groups(two, [(1, 0), (2, 3)])
        return [left, one, two, three, relayed]

    slots = [spread(left) for left in lefts]
    rights = [right] + [along_rows(right, m) for m in range(1, rows)]
    weights = prepare_weights(project_weight, hidden_weight, final_weight, width)
    rt = turn(rights, residues, width)
    vectors = [v.reshape(1, -1) for v in (project_bias, pair_gain, pair_bias, hidden_bias, final_bias)]

    out = None
    for chunk in range(chunks):
        routed = route(place, rows, slots[chunk])
        mine = [routed[0]] + [along_rows(routed[m], m) for m in range(1, rows)]
        packed = pack(mine)
        blocks = [packed] + [along_members(packed, n) for n in range(1, fold)]
        calls = [[n] for n in range(fold)] if chunk == chunks - 1 else [list(range(fold))]
        for members in calls:
            out = pair_update(
                place, members, chunk, [blocks[n] for n in members], rt, weights, vectors, pair_state, out, width
            )
    return out


def solution(mesh):
    placed = (
        P("row", "col", None),
        P(),
        P(),
        P(),
        P(),
        P(),
        P(),
        P("row", "col", None),
        P(),
        P(),
        P(),
        P(),
        P(),
        P(),
    )

    return jax.shard_map(on_device, mesh=mesh, in_specs=placed, out_specs=P("row", "col", None), check_vma=False)
```

```python
import functools

import jax
import jax.numpy as jnp
from jax import lax
from jax.experimental import pallas as pl
from jax.experimental.pallas import tpu as pltpu
from jax.sharding import PartitionSpec as P


LANES = 128
VMEM = 16 * 2**20
EPS = 1e-05
F32 = jnp.float32
BF16 = jnp.bfloat16


def split(values):
    high = values.astype(BF16)
    low = (values - high.astype(F32)).astype(BF16)
    return high, low


def dot(a, b):
    return jnp.dot(a, b, preferred_element_type=F32)


def norm(values, gain, offset):
    middle = jnp.mean(values, axis=-1, keepdims=True)
    centred = values - middle
    spread = jnp.mean(jnp.square(centred), axis=-1, keepdims=True)
    return centred * lax.rsqrt(spread + EPS) * gain + offset


def project_kernel(seqs, residues, width, chunks, shift_ref, member_ref, x_hbm, gain_hbm, bias_hbm, lw_hbm, rw_hbm, *refs):
    left_refs, right_ref = refs[:chunks], refs[chunks]
    x_ref, gain_ref, bias_ref, lw_ref, rw_ref, sems, w_ref, p_ref = refs[chunks + 1 :]
    channels = x_ref.shape[1]
    per = LANES // width
    groups = residues // per
    block = seqs * residues
    steps = x_ref.shape[0] // block

    small = ((lw_hbm, lw_ref), (rw_hbm, rw_ref), (gain_hbm, gain_ref), (bias_hbm, bias_ref))
    copies = [pltpu.make_async_copy(a, b, sems.at[n]) for n, (a, b) in enumerate(small)]
    for step in range(steps):
        rows = pl.ds(step * block, block)
        copies.append(pltpu.make_async_copy(x_hbm.at[rows], x_ref.at[rows], sems.at[len(small) + step]))
    for copy in copies:
        copy.start()
    for copy in copies[: len(small)]:
        copy.wait()
    plain = jnp.concatenate([lw_ref[...], rw_ref[...]], axis=0)
    high, low = split(jnp.concatenate([plain * gain_ref[...], plain], axis=0).T)
    w_ref[:, :LANES] = high
    w_ref[:, LANES:] = low

    def multiply(values):
        high, low = split(values)
        both = dot(high, w_ref[...])
        return both[:, :LANES] + both[:, LANES:] + dot(low, w_ref[:, :LANES])

    offset = multiply(jnp.broadcast_to(bias_ref[...], (8, channels)))
    offset = pltpu.roll(offset, LANES - 2 * width, 1)[:1]
    lane = lax.broadcasted_iota(jnp.int32, (seqs, LANES), 1) // width
    share = groups // chunks
    for step in range(steps):
        copies[len(small) + step].wait()
        x = x_ref[step * block : (step + 1) * block, :]
        centred = x - jnp.mean(x, axis=-1, keepdims=True)
        spread = jnp.mean(jnp.square(centred), axis=-1, keepdims=True)
        p_ref[step] = multiply(centred) * lax.rsqrt(spread + EPS) + offset
        to = slice(step * seqs, (step + 1) * seqs)
        for g in range(groups):
            rows = [p_ref[step, pl.ds(g * per + e, seqs, stride=residues), :] for e in range(per)]
            for side in range(2):
                value = None
                for e in range(per):
                    shift = (e - side) % per * width
                    placed = pltpu.roll(rows[e], shift, 1) if shift else rows[e]
                    value = placed if value is None else jnp.where(lane == e, placed, value)
                if side:
                    right_ref[to, g * LANES : (g + 1) * LANES] = value
                else:
                    at = g % share
                    left_refs[g // share][to, at * LANES : (at + 1) * LANES] = value


def project(place, alignment, gain, bias, left_weight, right_weight, chunks):
    seq_local, residues, channels = alignment.shape
    width = left_weight.shape[1]
    steps = 4
    seqs = seq_local // steps
    span = residues * width
    outs = [jax.ShapeDtypeStruct((seq_local, span // chunks), F32)] * chunks + [
        jax.ShapeDtypeStruct((seq_local, span), F32),
    ]
    return pl.pallas_call(
        functools.partial(project_kernel, seqs, residues, width, chunks),
        out_shape=outs,
        in_specs=[pl.BlockSpec(memory_space=pltpu.SMEM)] * 2 + [pl.BlockSpec(memory_space=pltpu.HBM)] * 5,
        out_specs=[pl.BlockSpec(memory_space=pltpu.VMEM)] * len(outs),
        scratch_shapes=[
            pltpu.VMEM((seq_local * residues, channels), F32),
            pltpu.VMEM((1, channels), F32),
            pltpu.VMEM((1, channels), F32),
            pltpu.VMEM((width, channels), F32),
            pltpu.VMEM((width, channels), F32),
            pltpu.SemaphoreType.DMA((4 + steps,)),
            pltpu.VMEM((channels, 2 * LANES), BF16),
            pltpu.VMEM((steps, seqs * residues, LANES), F32),
        ],
        cost_estimate=pl.CostEstimate(flops=6 * 10**9, bytes_accessed=4 * 10**6, transcendentals=0),
        compiler_params=pltpu.CompilerParams(vmem_limit_bytes=VMEM),
        name="project",
    )(
        *place,
        *(
            pltpu.with_memory_space_constraint(a, pltpu.HBM)
            for a in (
                alignment.reshape(seq_local * residues, channels),
                gain.reshape(1, channels),
                bias.reshape(1, channels),
                left_weight.T,
                right_weight.T,
            )
        )
    )


def weights_kernel(width, wp_ref, wh_ref, wf_ref, wp_out, wh_out, wf_out):
    pair = wp_ref.shape[1]
    for d in range(width):
        high, low = split(wp_ref[pl.ds(d, width, stride=width), :])
        wp_out[d * width : (d + 1) * width, :pair] = high
        wp_out[d * width : (d + 1) * width, pair:] = low
    high, low = split(wh_ref[...])
    wh_out[:pair] = high
    wh_out[pair : 2 * pair] = high
    wh_out[2 * pair :] = low
    high, low = split(wf_ref[...])
    wf_out[:, :pair] = high
    wf_out[:, pair:] = low


def prepare_weights(project_weight, hidden_weight, final_weight, width):
    pair, hidden = hidden_weight.shape
    return pl.pallas_call(
        functools.partial(weights_kernel, width),
        out_shape=[
            jax.ShapeDtypeStruct((width * width, 2 * pair), BF16),
            jax.ShapeDtypeStruct((3 * pair, hidden), BF16),
            jax.ShapeDtypeStruct((hidden, 2 * pair), BF16),
        ],
        cost_estimate=pl.CostEstimate(flops=10**9, bytes_accessed=2 * 10**6, transcendentals=0),
        compiler_params=pltpu.CompilerParams(vmem_limit_bytes=VMEM),
        name="weights",
    )(project_weight, hidden_weight, final_weight)


def turn_kernel(residues, width, scale, *refs):
    parts, out_ref, turned = refs[:-2], refs[-2], refs[-1]
    seqs = parts[0].shape[0]
    total = seqs * len(parts)
    whole = jnp.concatenate([p[...] for p in parts], axis=0) * scale
    for part in range(total // LANES):
        turned[part] = whole[part * LANES : (part + 1) * LANES].T
    for d in range(width):
        rows = slice(d * residues, (d + 1) * residues)
        for part in range(total // LANES):
            high, low = split(turned[part, pl.ds(d, residues, stride=width), :])
            for at, value in ((0, high), (total, low), (2 * total, high)):
                first = at + part * LANES
                out_ref[rows, first : first + LANES] = value


def turn(parts, residues, width):
    seqs, span = parts[0].shape
    total = seqs * len(parts)
    return pl.pallas_call(
        functools.partial(turn_kernel, residues, width, 1.0 / total),
        out_shape=jax.ShapeDtypeStruct((span, 3 * total), BF16),
        scratch_shapes=[pltpu.VMEM((total // LANES, span, LANES), F32)],
        cost_estimate=pl.CostEstimate(flops=2 * 10**9, bytes_accessed=3 * 10**6, transcendentals=0),
        compiler_params=pltpu.CompilerParams(vmem_limit_bytes=VMEM),
        name="turn",
    )(*parts)


def route_kernel(slots, t_ref, *refs):
    ins, outs = refs[:-slots], refs[-slots:]
    for t in range(slots):

        @pl.when(t_ref[0] == t)
        def _():
            for m in range(slots):
                outs[m][...] = ins[m ^ t][...]


def route(t, slots, ins):
    spec = pl.BlockSpec(memory_space=pltpu.VMEM)
    return pl.pallas_call(
        functools.partial(route_kernel, slots),
        out_shape=[jax.ShapeDtypeStruct(ins[0].shape, F32)] * slots,
        in_specs=[pl.BlockSpec(memory_space=pltpu.SMEM)] + [spec] * len(ins),
        out_specs=[spec] * slots,
        cost_estimate=pl.CostEstimate(flops=10**6, bytes_accessed=2 * 10**6, transcendentals=0),
        compiler_params=pltpu.CompilerParams(vmem_limit_bytes=VMEM),
        name="route",
    )(t, *ins)


def pack_kernel(*refs):
    rows = refs[0].shape[0]
    for n, ref in enumerate(refs[:-1]):
        refs[-1][n * rows : (n + 1) * rows, :] = ref[...]


def pack(parts):
    rows, span = parts[0].shape
    return pl.pallas_call(
        pack_kernel,
        out_shape=jax.ShapeDtypeStruct((rows * len(parts), span), F32),
        cost_estimate=pl.CostEstimate(flops=10**6, bytes_accessed=10**6, transcendentals=0),
        compiler_params=pltpu.CompilerParams(vmem_limit_bytes=VMEM),
        name="pack",
    )(*parts)


def pair_kernel(parts, steps, tile, width, at_ref, *refs):
    l_refs = refs[:parts]
    rt_ref, wp_ref, wh_ref, wf_ref, pb_ref, pg_ref, po_ref, hb_ref, fb_ref, ps_ref = refs[parts : parts + 10]
    out_ref, high_ref, low_ref = refs[-3:]
    residues, pair = ps_ref.shape[1:]
    per = LANES // width
    left = l_refs[0][...]
    for n in range(1, parts):
        left = jnp.where(pl.program_id(0) >= n * steps, l_refs[n][...], left)
    high, low = split(left)
    left = jnp.concatenate([high, high, low], axis=0)
    lane = lax.broadcasted_iota(jnp.int32, (residues, LANES), 1) // width
    odd, upper = lane % 2 == 1, lane >= 2
    block = 2 * per
    for first in range(0, width, block):
        outer = dot(rt_ref[first * residues : (first + block) * residues, :], left)
        for d0 in range(0, block, per):
            for g in range(tile // per):
                u = []
                for d in range(per):
                    rows = (d0 + d) * residues
                    v = outer[rows : rows + residues, g * LANES : (g + 1) * LANES]
                    u.append(pltpu.roll(v, d * width, 1) if d else v)
                x = [jnp.where(odd, u[(n + 1) % per], u[n]) for n in range(per)]
                for i in range(per):
                    n = -i % per
                    y = jnp.where(upper, x[(n + 2) % per], x[n])
                    y = pltpu.roll(y, (per - i) * width, 1) if i else y
                    high, low = split(y)
                    rows = slice((g * per + i) * residues, (g * per + i + 1) * residues)
                    lanes = slice((first + d0) * width, (first + d0 + per) * width)
                    high_ref[rows, lanes] = high
                    low_ref[rows, lanes] = low
    both = dot(high_ref[...], wp_ref[...])
    update = both[:, :pair] + both[:, pair:] + dot(low_ref[...], wp_ref[:, :pair])
    updated = ps_ref[...].reshape(tile * residues, pair) + update + pb_ref[...]
    high, low = split(norm(updated, pg_ref[...], po_ref[...]))
    hidden = jnp.maximum(dot(jnp.concatenate([high, low, high], axis=1), wh_ref[...]) + hb_ref[...], 0.0)
    high, low = split(hidden)
    both = dot(high, wf_ref[...])
    output = both[:, :pair] + both[:, pair:] + dot(low, wf_ref[:, :pair]) + fb_ref[...]
    out_ref[...] = (updated + output).reshape(tile, residues, pair)


def pair_update(place, members, chunk, lefts, rt, weights, vectors, pair_state, out, width):
    tile = 16
    wp, wh, wf = weights
    seqs, span = lefts[0].shape
    steps = span // (tile * width)
    residues, pair = pair_state.shape[1:]
    whole = lambda a: pl.BlockSpec(a.shape, lambda s, at: (0,) * a.ndim, pipeline_mode=pl.Buffered(1))
    tiles = residues // tile

    def tile_at(s, place):
        member = jnp.bitwise_xor(place[0], members[0])
        for n in range(1, len(members)):
            member = jnp.where(s >= n * steps, jnp.bitwise_xor(place[0], members[n]), member)
        return member * tiles + chunk * steps + lax.rem(s, steps), 0, 0

    rows = pl.BlockSpec((tile, residues, pair), tile_at)
    fixed = [pltpu.with_memory_space_constraint(a, pltpu.VMEM) for a in (rt, wp, wh, wf)]
    operands = [*lefts, *fixed, *vectors, pair_state]
    specs = [
        pl.BlockSpec((seqs, tile * width), lambda s, at, n=n: (0, jnp.clip(s - n * steps, 0, steps - 1)))
        for n in range(len(lefts))
    ]
    specs += [whole(a) for a in operands[len(lefts) : -1]] + [rows]
    aliases = {}
    if out is not None:
        aliases = {len(operands) + 1: 0}
        operands.append(out)
        specs.append(pl.BlockSpec(memory_space=pl.ANY))
    return pl.pallas_call(
        functools.partial(pair_kernel, len(lefts), steps, tile, width),
        out_shape=jax.ShapeDtypeStruct(pair_state.shape, F32),
        grid_spec=pltpu.PrefetchScalarGridSpec(
            num_scalar_prefetch=1,
            grid=(steps * len(lefts),),
            in_specs=specs,
            out_specs=rows,
            scratch_shapes=[
                pltpu.VMEM((tile * residues, width * width), BF16),
                pltpu.VMEM((tile * residues, width * width), BF16),
            ],
        ),
        input_output_aliases=aliases,
        cost_estimate=pl.CostEstimate(flops=steps * len(lefts) * 10**9, bytes_accessed=4 * 10**6, transcendentals=0),
        compiler_params=pltpu.CompilerParams(vmem_limit_bytes=VMEM),
        name="pair",
    )(place, *operands)


def on_device(
    alignment,
    align_gain,
    align_bias,
    left_weight,
    right_weight,
    project_weight,
    project_bias,
    pair_state,
    pair_gain,
    pair_bias,
    hidden_weight,
    hidden_bias,
    final_weight,
    final_bias,
):
    chunks = 2
    residues = alignment.shape[1]
    width = left_weight.shape[1]
    rows = lax.axis_size("row")
    cols = lax.axis_size("col")
    fold = cols // rows

    def along_groups(value, pairs):
        return lax.ppermute(value, "col", [(a * fold + k, b * fold + k) for a, b in pairs for k in range(fold)])

    def along_rows(value, m):
        return lax.ppermute(value, "row", [(a, a ^ m) for a in range(rows)])

    def along_members(value, n):
        return lax.ppermute(value, "col", [(a, a ^ n) for a in range(cols)])

    col = lax.axis_index("col")
    shift = jnp.bitwise_xor(lax.div(col, fold), lax.axis_index("row")).astype(jnp.int32).reshape(1)
    member = lax.rem(col, fold).astype(jnp.int32).reshape(1)
    *lefts, right = project((shift, member), alignment, align_gain, align_bias, left_weight, right_weight, chunks)

    def spread(left):
        return [left] + [along_groups(left, [(a, a ^ m) for a in range(rows)]) for m in range(1, rows)]

    slots = [spread(left) for left in lefts]
    rights = [right] + [along_rows(right, m) for m in range(1, rows)]
    weights = prepare_weights(project_weight, hidden_weight, final_weight, width)
    rt = turn(rights, residues, width)
    vectors = [v.reshape(1, -1) for v in (project_bias, pair_gain, pair_bias, hidden_bias, final_bias)]

    out = None
    for chunk in range(chunks):
        routed = route(shift, rows, slots[chunk])
        mine = [routed[0]] + [along_rows(routed[m], m) for m in range(1, rows)]
        packed = pack(mine)
        blocks = [packed] + [along_members(packed, n) for n in range(1, fold)]
        for n in range(fold):
            out = pair_update(member, [n], chunk, [blocks[n]], rt, weights, vectors, pair_state, out, width)
    return out


def solution(mesh):
    placed = (
        P("row", "col", None),
        P(),
        P(),
        P(),
        P(),
        P(),
        P(),
        P("row", "col", None),
        P(),
        P(),
        P(),
        P(),
        P(),
        P(),
    )

    return jax.shard_map(on_device, mesh=mesh, in_specs=placed, out_specs=P("row", "col", None), check_vma=False)
```

```python
import functools

import jax
import jax.numpy as jnp
from jax import lax
from jax.experimental import pallas as pl
from jax.experimental.pallas import tpu as pltpu
from jax.sharding import PartitionSpec as P


LANES = 128
VMEM = 16 * 2**20
EPS = 1e-05
F32 = jnp.float32
BF16 = jnp.bfloat16


def split(values):
    high = values.astype(BF16)
    low = (values - high.astype(F32)).astype(BF16)
    return high, low


def dot(a, b):
    return jnp.dot(a, b, preferred_element_type=F32)


def norm(values, gain, offset):
    middle = jnp.mean(values, axis=-1, keepdims=True)
    centred = values - middle
    spread = jnp.mean(jnp.square(centred), axis=-1, keepdims=True)
    return centred * lax.rsqrt(spread + EPS) * gain + offset


def project_kernel(chunk, steps, width, shift_ref, member_ref, x_hbm, *refs):
    if chunk:
        w_ref, offset_ref, before_ref, left_ref, right_ref, p_ref = refs
        x_ref = x_hbm
    else:
        gain_hbm, bias_hbm, lw_hbm, rw_hbm, *refs = refs
        left_ref, right_ref, w_ref, offset_ref, rest_ref, p_ref, x_ref, sems, gain_ref, bias_ref, lw_ref, rw_ref = refs
        small = ((lw_hbm, lw_ref), (rw_hbm, rw_ref), (gain_hbm, gain_ref), (bias_hbm, bias_ref))
    seq_local, residues, channels = x_ref.shape
    seqs = seq_local // steps
    per = LANES // width
    groups = residues // per

    if not chunk:
        copies = [pltpu.make_async_copy(a, b, sems.at[steps + n]) for n, (a, b) in enumerate(small)]
        blocks = []
        for step in range(steps):
            rows = pl.ds(step * seqs, seqs)
            blocks.append(
                pltpu.make_async_copy(x_hbm.at[rows, pl.ds(0, residues)], x_ref.at[rows], sems.at[step])
            )
        rest = x_hbm.at[:, pl.ds(residues, rest_ref.shape[1])]
        rest = pltpu.make_async_copy(rest, rest_ref, sems.at[steps + len(small)])
        for copy in copies + blocks + [rest]:
            copy.start()
        for copy in copies:
            copy.wait()

    def multiply(values):
        high, low = split(values)
        both = dot(high, w_ref[...])
        return both[:, :LANES] + both[:, LANES:] + dot(low, w_ref[:, :LANES])

    if chunk:
        right_ref[:, : chunk * residues * width] = before_ref[...]
    else:
        plain = jnp.concatenate([lw_ref[...], rw_ref[...]], axis=0)
        high, low = split(jnp.concatenate([plain * gain_ref[...], plain], axis=0).T)
        w_ref[:, :LANES] = high
        w_ref[:, LANES:] = low
        offset_ref[...] = pltpu.roll(multiply(jnp.broadcast_to(bias_ref[...], (8, channels))), LANES - 2 * width, 1)
    offset = offset_ref[:1]
    lane = lax.broadcasted_iota(jnp.int32, (seqs, LANES), 1) // width

    def product(step):
        x = x_ref[step * seqs : (step + 1) * seqs].reshape(seqs * residues, channels)
        centred = x - jnp.mean(x, axis=-1, keepdims=True)
        spread = jnp.mean(jnp.square(centred), axis=-1, keepdims=True)
        p_ref[step] = multiply(centred) * lax.rsqrt(spread + EPS) + offset

    def place(step):
        to = slice(step * seqs, (step + 1) * seqs)
        for g in range(groups):
            rows = [p_ref[step, pl.ds(g * per + e, seqs, stride=residues), :] for e in range(per)]
            for side, ref, at in ((0, left_ref, g), (1, right_ref, chunk * groups + g)):
                value = None
                for e in range(per):
                    turn = (e - side) % per * width
                    placed = pltpu.roll(rows[e], turn, 1) if turn else rows[e]
                    value = placed if value is None else jnp.where(lane == e, placed, value)
                ref[to, at * LANES : (at + 1) * LANES] = value

    for step in range(steps):
        if not chunk:
            blocks[step].wait()
        product(step)
        if step:
            place(step - 1)
    place(steps - 1)
    if not chunk:
        rest.wait()


def project(scalars, alignment, residues, small, given, width):
    seq_local, left_over, channels = alignment.shape
    steps = 4
    span = residues * width
    vmem = pl.BlockSpec(memory_space=pltpu.VMEM)
    smem = pl.BlockSpec(memory_space=pltpu.SMEM)
    hbm = pl.BlockSpec(memory_space=pltpu.HBM)
    outs = [
        jax.ShapeDtypeStruct((seq_local, span), F32),
        jax.ShapeDtypeStruct((seq_local, span * (2 if given else 1)), F32),
    ]
    scratch = [pltpu.VMEM((steps, seq_local // steps * residues, LANES), F32)]
    if given:
        arrays = [alignment, *given]
        specs = [vmem] * len(arrays)
    else:
        arrays = [pltpu.with_memory_space_constraint(a, pltpu.HBM) for a in (alignment, *small)]
        specs = [hbm] * len(arrays)
        outs += [
            jax.ShapeDtypeStruct((channels, 2 * LANES), BF16),
            jax.ShapeDtypeStruct((8, LANES), F32),
            jax.ShapeDtypeStruct((seq_local, left_over - residues, channels), F32),
        ]
        scratch += [
            pltpu.VMEM((seq_local, residues, channels), F32),
            pltpu.SemaphoreType.DMA((steps + len(small) + 1,)),
        ]
        scratch += [pltpu.VMEM(a.shape, F32) for a in small]
    return pl.pallas_call(
        functools.partial(project_kernel, 1 if given else 0, steps, width),
        out_shape=outs,
        in_specs=[smem] * 2 + specs,
        out_specs=[vmem] * len(outs),
        scratch_shapes=scratch,
        cost_estimate=pl.CostEstimate(flops=3 * 10**9, bytes_accessed=2 * 10**6, transcendentals=0),
        compiler_params=pltpu.CompilerParams(vmem_limit_bytes=VMEM),
        name="project",
    )(*scalars, *arrays)


def weights_kernel(width, wp_ref, wh_ref, wf_ref, wp_out, wh_out, wf_out):
    pair = wp_ref.shape[1]
    for d in range(width):
        high, low = split(wp_ref[pl.ds(d, width, stride=width), :])
        wp_out[d * width : (d + 1) * width, :pair] = high
        wp_out[d * width : (d + 1) * width, pair:] = low
    high, low = split(wh_ref[...])
    wh_out[:pair] = high
    wh_out[pair : 2 * pair] = high
    wh_out[2 * pair :] = low
    high, low = split(wf_ref[...])
    wf_out[:, :pair] = high
    wf_out[:, pair:] = low


def prepare_weights(project_weight, hidden_weight, final_weight, width):
    pair, hidden = hidden_weight.shape
    return pl.pallas_call(
        functools.partial(weights_kernel, width),
        out_shape=[
            jax.ShapeDtypeStruct((width * width, 2 * pair), BF16),
            jax.ShapeDtypeStruct((3 * pair, hidden), BF16),
            jax.ShapeDtypeStruct((hidden, 2 * pair), BF16),
        ],
        cost_estimate=pl.CostEstimate(flops=10**9, bytes_accessed=2 * 10**6, transcendentals=0),
        compiler_params=pltpu.CompilerParams(vmem_limit_bytes=VMEM),
        name="weights",
    )(project_weight, hidden_weight, final_weight)


def turn_kernel(residues, width, scale, *refs):
    parts, out_ref, turned = refs[:-2], refs[-2], refs[-1]
    seqs = parts[0].shape[0]
    total = seqs * len(parts)
    whole = jnp.concatenate([p[...] for p in parts], axis=0) * scale
    for part in range(total // LANES):
        turned[part] = whole[part * LANES : (part + 1) * LANES].T
    for d in range(width):
        rows = slice(d * residues, (d + 1) * residues)
        for part in range(total // LANES):
            high, low = split(turned[part, pl.ds(d, residues, stride=width), :])
            for at, value in ((0, high), (total, low), (2 * total, high)):
                first = at + part * LANES
                out_ref[rows, first : first + LANES] = value


def turn(parts, residues, width):
    seqs, span = parts[0].shape
    total = seqs * len(parts)
    return pl.pallas_call(
        functools.partial(turn_kernel, residues, width, 1.0 / total),
        out_shape=jax.ShapeDtypeStruct((span, 3 * total), BF16),
        scratch_shapes=[pltpu.VMEM((total // LANES, span, LANES), F32)],
        cost_estimate=pl.CostEstimate(flops=2 * 10**9, bytes_accessed=3 * 10**6, transcendentals=0),
        compiler_params=pltpu.CompilerParams(vmem_limit_bytes=VMEM),
        name="turn",
    )(*parts)


def route_kernel(slots, t_ref, *refs):
    ins, outs = refs[:-slots], refs[-slots:]
    for t in range(slots):

        @pl.when(t_ref[0] == t)
        def _():
            for m in range(slots):
                outs[m][...] = ins[m ^ t][...]


def route(t, slots, ins):
    spec = pl.BlockSpec(memory_space=pltpu.VMEM)
    return pl.pallas_call(
        functools.partial(route_kernel, slots),
        out_shape=[jax.ShapeDtypeStruct(ins[0].shape, F32)] * slots,
        in_specs=[pl.BlockSpec(memory_space=pltpu.SMEM)] + [spec] * len(ins),
        out_specs=[spec] * slots,
        cost_estimate=pl.CostEstimate(flops=10**6, bytes_accessed=2 * 10**6, transcendentals=0),
        compiler_params=pltpu.CompilerParams(vmem_limit_bytes=VMEM),
        name="route",
    )(t, *ins)


def pack_kernel(*refs):
    rows = refs[0].shape[0]
    for n, ref in enumerate(refs[:-1]):
        refs[-1][n * rows : (n + 1) * rows, :] = ref[...]


def pack(parts):
    rows, span = parts[0].shape
    return pl.pallas_call(
        pack_kernel,
        out_shape=jax.ShapeDtypeStruct((rows * len(parts), span), F32),
        cost_estimate=pl.CostEstimate(flops=10**6, bytes_accessed=10**6, transcendentals=0),
        compiler_params=pltpu.CompilerParams(vmem_limit_bytes=VMEM),
        name="pack",
    )(*parts)


def pair_kernel(parts, steps, tile, width, at_ref, *refs):
    l_refs = refs[:parts]
    rt_ref, wp_ref, wh_ref, wf_ref, pb_ref, pg_ref, po_ref, hb_ref, fb_ref, ps_ref = refs[parts : parts + 10]
    out_ref, high_ref, low_ref = refs[-3:]
    residues, pair = ps_ref.shape[1:]
    per = LANES // width
    left = l_refs[0][...]
    for n in range(1, parts):
        left = jnp.where(pl.program_id(0) >= n * steps, l_refs[n][...], left)
    high, low = split(left)
    left = jnp.concatenate([high, high, low], axis=0)
    lane = lax.broadcasted_iota(jnp.int32, (residues, LANES), 1) // width
    odd, upper = lane % 2 == 1, lane >= 2
    block = 2 * per
    for first in range(0, width, block):
        outer = dot(rt_ref[first * residues : (first + block) * residues, :], left)
        for d0 in range(0, block, per):
            for g in range(tile // per):
                u = []
                for d in range(per):
                    rows = (d0 + d) * residues
                    v = outer[rows : rows + residues, g * LANES : (g + 1) * LANES]
                    u.append(pltpu.roll(v, d * width, 1) if d else v)
                x = [jnp.where(odd, u[(n + 1) % per], u[n]) for n in range(per)]
                for i in range(per):
                    n = -i % per
                    y = jnp.where(upper, x[(n + 2) % per], x[n])
                    y = pltpu.roll(y, (per - i) * width, 1) if i else y
                    high, low = split(y)
                    rows = slice((g * per + i) * residues, (g * per + i + 1) * residues)
                    lanes = slice((first + d0) * width, (first + d0 + per) * width)
                    high_ref[rows, lanes] = high
                    low_ref[rows, lanes] = low
    both = dot(high_ref[...], wp_ref[...])
    update = both[:, :pair] + both[:, pair:] + dot(low_ref[...], wp_ref[:, :pair])
    updated = ps_ref[...].reshape(tile * residues, pair) + update + pb_ref[...]
    high, low = split(norm(updated, pg_ref[...], po_ref[...]))
    hidden = jnp.maximum(dot(jnp.concatenate([high, low, high], axis=1), wh_ref[...]) + hb_ref[...], 0.0)
    high, low = split(hidden)
    both = dot(high, wf_ref[...])
    output = both[:, :pair] + both[:, pair:] + dot(low, wf_ref[:, :pair]) + fb_ref[...]
    out_ref[...] = (updated + output).reshape(tile, residues, pair)


def pair_update(place, members, chunk, lefts, rt, weights, vectors, pair_state, out, width):
    tile = 16
    wp, wh, wf = weights
    seqs, span = lefts[0].shape
    steps = span // (tile * width)
    residues, pair = pair_state.shape[1:]
    whole = lambda a: pl.BlockSpec(a.shape, lambda s, at: (0,) * a.ndim, pipeline_mode=pl.Buffered(1))
    tiles = residues // tile

    def tile_at(s, place):
        member = jnp.bitwise_xor(place[0], members[0])
        for n in range(1, len(members)):
            member = jnp.where(s >= n * steps, jnp.bitwise_xor(place[0], members[n]), member)
        return member * tiles + chunk * steps + lax.rem(s, steps), 0, 0

    rows = pl.BlockSpec((tile, residues, pair), tile_at)
    fixed = [pltpu.with_memory_space_constraint(a, pltpu.VMEM) for a in (rt, wp, wh, wf)]
    operands = [*lefts, *fixed, *vectors, pair_state]
    specs = [
        pl.BlockSpec((seqs, tile * width), lambda s, at, n=n: (0, jnp.clip(s - n * steps, 0, steps - 1)))
        for n in range(len(lefts))
    ]
    specs += [whole(a) for a in operands[len(lefts) : -1]] + [rows]
    aliases = {}
    if out is not None:
        aliases = {len(operands) + 1: 0}
        operands.append(out)
        specs.append(pl.BlockSpec(memory_space=pl.ANY))
    return pl.pallas_call(
        functools.partial(pair_kernel, len(lefts), steps, tile, width),
        out_shape=jax.ShapeDtypeStruct(pair_state.shape, F32),
        grid_spec=pltpu.PrefetchScalarGridSpec(
            num_scalar_prefetch=1,
            grid=(steps * len(lefts),),
            in_specs=specs,
            out_specs=rows,
            scratch_shapes=[
                pltpu.VMEM((tile * residues, width * width), BF16),
                pltpu.VMEM((tile * residues, width * width), BF16),
            ],
        ),
        input_output_aliases=aliases,
        cost_estimate=pl.CostEstimate(flops=steps * len(lefts) * 10**9, bytes_accessed=4 * 10**6, transcendentals=0),
        compiler_params=pltpu.CompilerParams(vmem_limit_bytes=VMEM),
        name="pair",
    )(place, *operands)


def on_device(
    alignment,
    align_gain,
    align_bias,
    left_weight,
    right_weight,
    project_weight,
    project_bias,
    pair_state,
    pair_gain,
    pair_bias,
    hidden_weight,
    hidden_bias,
    final_weight,
    final_bias,
):
    chunks = 2
    residues = alignment.shape[1]
    width = left_weight.shape[1]
    rows = lax.axis_size("row")
    cols = lax.axis_size("col")
    fold = cols // rows

    def along_groups(value, pairs):
        return lax.ppermute(value, "col", [(a * fold + k, b * fold + k) for a, b in pairs for k in range(fold)])

    def along_rows(value, m):
        return lax.ppermute(value, "row", [(a, a ^ m) for a in range(rows)])

    def along_members(value, n):
        return lax.ppermute(value, "col", [(a, a ^ n) for a in range(cols)])

    col = lax.axis_index("col")
    shift = jnp.bitwise_xor(lax.div(col, fold), lax.axis_index("row")).astype(jnp.int32).reshape(1)
    member = lax.rem(col, fold).astype(jnp.int32).reshape(1)
    small = (align_gain.reshape(1, -1), align_bias.reshape(1, -1), left_weight.T, right_weight.T)
    scalars = (shift, member)
    part = residues // chunks
    first, right, *shared, rest = project(scalars, alignment, part, small, (), width)
    second, right = project(scalars, rest, part, (), (*shared, right), width)
    lefts = [first, second]

    def spread(left):
        return [left] + [along_groups(left, [(a, a ^ m) for a in range(rows)]) for m in range(1, rows)]

    slots = [spread(left) for left in lefts]
    rights = [right] + [along_rows(right, m) for m in range(1, rows)]
    weights = prepare_weights(project_weight, hidden_weight, final_weight, width)
    rt = turn(rights, residues, width)
    vectors = [v.reshape(1, -1) for v in (project_bias, pair_gain, pair_bias, hidden_bias, final_bias)]

    out = None
    for chunk in range(chunks):
        routed = route(shift, rows, slots[chunk])
        mine = [routed[0]] + [along_rows(routed[m], m) for m in range(1, rows)]
        packed = pack(mine)
        blocks = [packed] + [along_members(packed, n) for n in range(1, fold)]
        for n in range(fold):
            out = pair_update(member, [n], chunk, [blocks[n]], rt, weights, vectors, pair_state, out, width)
    return out


def solution(mesh):
    placed = (
        P("row", "col", None),
        P(),
        P(),
        P(),
        P(),
        P(),
        P(),
        P("row", "col", None),
        P(),
        P(),
        P(),
        P(),
        P(),
        P(),
    )

    return jax.shard_map(on_device, mesh=mesh, in_specs=placed, out_specs=P("row", "col", None), check_vma=False)
```

```python
import functools

import jax
import jax.numpy as jnp
from jax import lax
from jax.experimental import pallas as pl
from jax.experimental.pallas import tpu as pltpu
from jax.sharding import PartitionSpec as P


LANES = 128
VMEM = 16 * 2**20
EPS = 1e-05
F32 = jnp.float32
BF16 = jnp.bfloat16


def split(values):
    high = values.astype(BF16)
    low = (values - high.astype(F32)).astype(BF16)
    return high, low


def dot(a, b):
    return jnp.dot(a, b, preferred_element_type=F32)


def norm(values, gain, offset):
    middle = jnp.mean(values, axis=-1, keepdims=True)
    centred = values - middle
    spread = jnp.mean(jnp.square(centred), axis=-1, keepdims=True)
    return centred * lax.rsqrt(spread + EPS) * gain + offset


def project_kernel(chunk, steps, width, shift_ref, member_ref, x_hbm, *refs):
    if chunk:
        w_ref, offset_ref, before_ref, left_ref, right_ref, p_ref = refs
        x_ref = x_hbm
    else:
        gain_hbm, bias_hbm, lw_hbm, rw_hbm, *refs = refs
        left_ref, right_ref, w_ref, offset_ref, rest_ref, p_ref, x_ref, sems, gain_ref, bias_ref, lw_ref, rw_ref = refs
        small = ((lw_hbm, lw_ref), (rw_hbm, rw_ref), (gain_hbm, gain_ref), (bias_hbm, bias_ref))
    seq_local, residues, channels = x_ref.shape
    seqs = seq_local // steps
    per = LANES // width
    groups = residues // per

    if not chunk:
        copies = [pltpu.make_async_copy(a, b, sems.at[steps + n]) for n, (a, b) in enumerate(small)]
        blocks = []
        for step in range(steps):
            rows = pl.ds(step * seqs, seqs)
            blocks.append(
                pltpu.make_async_copy(x_hbm.at[rows, pl.ds(0, residues)], x_ref.at[rows], sems.at[step])
            )
        rest = x_hbm.at[:, pl.ds(residues, rest_ref.shape[1])]
        rest = pltpu.make_async_copy(rest, rest_ref, sems.at[steps + len(small)])
        for copy in copies + blocks + [rest]:
            copy.start()
        for copy in copies:
            copy.wait()

    def multiply(values):
        high, low = split(values)
        both = dot(high, w_ref[...])
        return both[:, :LANES] + both[:, LANES:] + dot(low, w_ref[:, :LANES])

    if chunk:
        right_ref[:, : chunk * residues * width] = before_ref[...]
    else:
        plain = jnp.concatenate([lw_ref[...], rw_ref[...]], axis=0)
        high, low = split(jnp.concatenate([plain * gain_ref[...], plain], axis=0).T)
        w_ref[:, :LANES] = high
        w_ref[:, LANES:] = low
        offset_ref[...] = pltpu.roll(multiply(jnp.broadcast_to(bias_ref[...], (8, channels))), LANES - 2 * width, 1)
    offset = offset_ref[:1]
    lane = lax.broadcasted_iota(jnp.int32, (seqs, LANES), 1) // width

    def product(step):
        x = x_ref[step * seqs : (step + 1) * seqs].reshape(seqs * residues, channels)
        centred = x - jnp.mean(x, axis=-1, keepdims=True)
        spread = jnp.mean(jnp.square(centred), axis=-1, keepdims=True)
        p_ref[step] = multiply(centred) * lax.rsqrt(spread + EPS) + offset

    def place(step):
        to = slice(step * seqs, (step + 1) * seqs)
        for g in range(groups):
            rows = [p_ref[step, pl.ds(g * per + e, seqs, stride=residues), :] for e in range(per)]
            for side, ref, at in ((0, left_ref, g), (1, right_ref, chunk * groups + g)):
                value = None
                for e in range(per):
                    turn = (e - side) % per * width
                    placed = pltpu.roll(rows[e], turn, 1) if turn else rows[e]
                    value = placed if value is None else jnp.where(lane == e, placed, value)
                ref[to, at * LANES : (at + 1) * LANES] = value

    for step in range(steps):
        if not chunk:
            blocks[step].wait()
        product(step)
        if step:
            place(step - 1)
    place(steps - 1)
    if not chunk:
        rest.wait()


def project(scalars, alignment, residues, small, given, width):
    seq_local, left_over, channels = alignment.shape
    steps = 2
    span = residues * width
    vmem = pl.BlockSpec(memory_space=pltpu.VMEM)
    smem = pl.BlockSpec(memory_space=pltpu.SMEM)
    hbm = pl.BlockSpec(memory_space=pltpu.HBM)
    outs = [
        jax.ShapeDtypeStruct((seq_local, span), F32),
        jax.ShapeDtypeStruct((seq_local, span * (2 if given else 1)), F32),
    ]
    scratch = [pltpu.VMEM((steps, seq_local // steps * residues, LANES), F32)]
    if given:
        arrays = [alignment, *given]
        specs = [vmem] * len(arrays)
    else:
        arrays = [pltpu.with_memory_space_constraint(a, pltpu.HBM) for a in (alignment, *small)]
        specs = [hbm] * len(arrays)
        outs += [
            jax.ShapeDtypeStruct((channels, 2 * LANES), BF16),
            jax.ShapeDtypeStruct((8, LANES), F32),
            jax.ShapeDtypeStruct((seq_local, left_over - residues, channels), F32),
        ]
        scratch += [
            pltpu.VMEM((seq_local, residues, channels), F32),
            pltpu.SemaphoreType.DMA((steps + len(small) + 1,)),
        ]
        scratch += [pltpu.VMEM(a.shape, F32) for a in small]
    return pl.pallas_call(
        functools.partial(project_kernel, 1 if given else 0, steps, width),
        out_shape=outs,
        in_specs=[smem] * 2 + specs,
        out_specs=[vmem] * len(outs),
        scratch_shapes=scratch,
        cost_estimate=pl.CostEstimate(flops=3 * 10**9, bytes_accessed=2 * 10**6, transcendentals=0),
        compiler_params=pltpu.CompilerParams(vmem_limit_bytes=VMEM),
        name="project",
    )(*scalars, *arrays)


def weights_kernel(width, wp_ref, wh_ref, wf_ref, wp_out, wh_out, wf_out):
    pair = wp_ref.shape[1]
    for d in range(width):
        high, low = split(wp_ref[pl.ds(d, width, stride=width), :])
        wp_out[d * width : (d + 1) * width, :pair] = high
        wp_out[d * width : (d + 1) * width, pair:] = low
    high, low = split(wh_ref[...])
    wh_out[:pair] = high
    wh_out[pair : 2 * pair] = high
    wh_out[2 * pair :] = low
    high, low = split(wf_ref[...])
    wf_out[:, :pair] = high
    wf_out[:, pair:] = low


def prepare_weights(project_weight, hidden_weight, final_weight, width):
    pair, hidden = hidden_weight.shape
    return pl.pallas_call(
        functools.partial(weights_kernel, width),
        out_shape=[
            jax.ShapeDtypeStruct((width * width, 2 * pair), BF16),
            jax.ShapeDtypeStruct((3 * pair, hidden), BF16),
            jax.ShapeDtypeStruct((hidden, 2 * pair), BF16),
        ],
        cost_estimate=pl.CostEstimate(flops=10**9, bytes_accessed=2 * 10**6, transcendentals=0),
        compiler_params=pltpu.CompilerParams(vmem_limit_bytes=VMEM),
        name="weights",
    )(project_weight, hidden_weight, final_weight)


def turn_kernel(residues, width, scale, *refs):
    parts, out_ref, turned = refs[:-2], refs[-2], refs[-1]
    seqs = parts[0].shape[0]
    total = seqs * len(parts)
    whole = jnp.concatenate([p[...] for p in parts], axis=0) * scale
    for part in range(total // LANES):
        turned[part] = whole[part * LANES : (part + 1) * LANES].T
    for d in range(width):
        rows = slice(d * residues, (d + 1) * residues)
        for part in range(total // LANES):
            high, low = split(turned[part, pl.ds(d, residues, stride=width), :])
            for at, value in ((0, high), (total, low), (2 * total, high)):
                first = at + part * LANES
                out_ref[rows, first : first + LANES] = value


def turn(parts, residues, width):
    seqs, span = parts[0].shape
    total = seqs * len(parts)
    return pl.pallas_call(
        functools.partial(turn_kernel, residues, width, 1.0 / total),
        out_shape=jax.ShapeDtypeStruct((span, 3 * total), BF16),
        scratch_shapes=[pltpu.VMEM((total // LANES, span, LANES), F32)],
        cost_estimate=pl.CostEstimate(flops=2 * 10**9, bytes_accessed=3 * 10**6, transcendentals=0),
        compiler_params=pltpu.CompilerParams(vmem_limit_bytes=VMEM),
        name="turn",
    )(*parts)


def route_kernel(slots, t_ref, *refs):
    ins, outs = refs[:-slots], refs[-slots:]
    for t in range(slots):

        @pl.when(t_ref[0] == t)
        def _():
            for m in range(slots):
                outs[m][...] = ins[m ^ t][...]


def route(t, slots, ins):
    spec = pl.BlockSpec(memory_space=pltpu.VMEM)
    return pl.pallas_call(
        functools.partial(route_kernel, slots),
        out_shape=[jax.ShapeDtypeStruct(ins[0].shape, F32)] * slots,
        in_specs=[pl.BlockSpec(memory_space=pltpu.SMEM)] + [spec] * len(ins),
        out_specs=[spec] * slots,
        cost_estimate=pl.CostEstimate(flops=10**6, bytes_accessed=2 * 10**6, transcendentals=0),
        compiler_params=pltpu.CompilerParams(vmem_limit_bytes=VMEM),
        name="route",
    )(t, *ins)


def pack_kernel(*refs):
    rows = refs[0].shape[0]
    for n, ref in enumerate(refs[:-1]):
        refs[-1][n * rows : (n + 1) * rows, :] = ref[...]


def pack(parts):
    rows, span = parts[0].shape
    return pl.pallas_call(
        pack_kernel,
        out_shape=jax.ShapeDtypeStruct((rows * len(parts), span), F32),
        cost_estimate=pl.CostEstimate(flops=10**6, bytes_accessed=10**6, transcendentals=0),
        compiler_params=pltpu.CompilerParams(vmem_limit_bytes=VMEM),
        name="pack",
    )(*parts)


def pair_kernel(places, part, width, member_ref, l_ref, rt_ref, wp_ref, wh_ref, wf_ref, *refs):
    pb_ref, pg_ref, po_ref, hb_ref, fb_ref, ps_ref, *refs = refs
    *earlier, out_ref, high_ref, low_ref = refs[: len(places) + 2]
    last = refs[len(places) + 2 :]
    residues, pair = ps_ref.shape[1:]
    per = LANES // width

    def rows_of(place):
        chunk, offset = place
        first = jnp.bitwise_xor(member_ref[0], offset) * residues + chunk * part
        return pl.ds(first, part)

    copies = []
    if last:
        own_ref, sems = last
        for n, (place, ref) in enumerate(zip(places, earlier)):
            copies.append(pltpu.make_async_copy(ref, out_ref.at[rows_of(place)], sems.at[n]))
            copies[-1].start()

    high, low = split(l_ref[...])
    left = jnp.concatenate([high, high, low], axis=0)
    lane = lax.broadcasted_iota(jnp.int32, (residues, LANES), 1) // width
    odd, upper = lane % 2 == 1, lane >= 2
    block = 2 * per
    for first in range(0, width, block):
        outer = dot(rt_ref[first * residues : (first + block) * residues, :], left)
        for d0 in range(0, block, per):
            for g in range(part // per):
                u = []
                for d in range(per):
                    rows = (d0 + d) * residues
                    v = outer[rows : rows + residues, g * LANES : (g + 1) * LANES]
                    u.append(pltpu.roll(v, d * width, 1) if d else v)
                x = [jnp.where(odd, u[(n + 1) % per], u[n]) for n in range(per)]
                for i in range(per):
                    n = -i % per
                    y = jnp.where(upper, x[(n + 2) % per], x[n])
                    y = pltpu.roll(y, (per - i) * width, 1) if i else y
                    high, low = split(y)
                    rows = slice((g * per + i) * residues, (g * per + i + 1) * residues)
                    lanes = slice((first + d0) * width, (first + d0 + per) * width)
                    high_ref[rows, lanes] = high
                    low_ref[rows, lanes] = low
    both = dot(high_ref[...], wp_ref[...])
    update = both[:, :pair] + both[:, pair:] + dot(low_ref[...], wp_ref[:, :pair])
    updated = ps_ref[rows_of(places[-1])].reshape(part * residues, pair) + update + pb_ref[...]
    high, low = split(norm(updated, pg_ref[...], po_ref[...]))
    hidden = jnp.maximum(dot(jnp.concatenate([high, low, high], axis=1), wh_ref[...]) + hb_ref[...], 0.0)
    high, low = split(hidden)
    both = dot(high, wf_ref[...])
    output = both[:, :pair] + both[:, pair:] + dot(low, wf_ref[:, :pair]) + fb_ref[...]
    result = (updated + output).reshape(part, residues, pair)
    if last:
        own_ref[...] = result
        copies.append(pltpu.make_async_copy(own_ref, out_ref.at[rows_of(places[-1])], sems.at[len(earlier)]))
        copies[-1].start()
        for copy in copies:
            copy.wait()
    else:
        out_ref[...] = result


def pair_update(member, places, left, rt, weights, vectors, pair_state, earlier, width):
    residues, pair = pair_state.shape[1:]
    part = left.shape[1] // width
    vmem = pl.BlockSpec(memory_space=pltpu.VMEM)
    operands = [left, rt, *weights, *vectors, pair_state, *earlier]
    operands = [pltpu.with_memory_space_constraint(a, pltpu.VMEM) for a in operands]
    scratch = [pltpu.VMEM((part * residues, width * width), BF16)] * 2
    block = (part, residues, pair)
    if earlier:
        scratch += [pltpu.VMEM(block, F32), pltpu.SemaphoreType.DMA((len(places),))]
    return pl.pallas_call(
        functools.partial(pair_kernel, places, part, width),
        out_shape=jax.ShapeDtypeStruct(pair_state.shape if earlier else block, F32),
        in_specs=[pl.BlockSpec(memory_space=pltpu.SMEM)] + [vmem] * len(operands),
        out_specs=pl.BlockSpec(memory_space=pltpu.HBM) if earlier else vmem,
        scratch_shapes=scratch,
        cost_estimate=pl.CostEstimate(flops=2 * 10**9, bytes_accessed=4 * 10**6, transcendentals=0),
        compiler_params=pltpu.CompilerParams(vmem_limit_bytes=VMEM),
        name="pair",
    )(member, *operands)


def on_device(
    alignment,
    align_gain,
    align_bias,
    left_weight,
    right_weight,
    project_weight,
    project_bias,
    pair_state,
    pair_gain,
    pair_bias,
    hidden_weight,
    hidden_bias,
    final_weight,
    final_bias,
):
    chunks = 2
    residues = alignment.shape[1]
    width = left_weight.shape[1]
    rows = lax.axis_size("row")
    cols = lax.axis_size("col")
    fold = cols // rows

    def along_groups(value, pairs):
        return lax.ppermute(value, "col", [(a * fold + k, b * fold + k) for a, b in pairs for k in range(fold)])

    def along_rows(value, m):
        return lax.ppermute(value, "row", [(a, a ^ m) for a in range(rows)])

    def along_members(value, n):
        return lax.ppermute(value, "col", [(a, a ^ n) for a in range(cols)])

    col = lax.axis_index("col")
    shift = jnp.bitwise_xor(lax.div(col, fold), lax.axis_index("row")).astype(jnp.int32).reshape(1)
    member = lax.rem(col, fold).astype(jnp.int32).reshape(1)
    small = (align_gain.reshape(1, -1), align_bias.reshape(1, -1), left_weight.T, right_weight.T)
    scalars = (shift, member)
    part = residues // chunks
    first, right, *shared, rest = project(scalars, alignment, part, small, (), width)
    second, right = project(scalars, rest, part, (), (*shared, right), width)
    lefts = [first, second]

    def spread(left):
        return [left] + [along_groups(left, [(a, a ^ m) for a in range(rows)]) for m in range(1, rows)]

    slots = [spread(left) for left in lefts]
    rights = [right] + [along_rows(right, m) for m in range(1, rows)]
    weights = prepare_weights(project_weight, hidden_weight, final_weight, width)
    rt = turn(rights, residues, width)
    vectors = [v.reshape(1, -1) for v in (project_bias, pair_gain, pair_bias, hidden_bias, final_bias)]

    places, results = [], []
    for chunk in range(chunks):
        routed = route(shift, rows, slots[chunk])
        mine = [routed[0]] + [along_rows(routed[m], m) for m in range(1, rows)]
        packed = pack(mine)
        blocks = [packed] + [along_members(packed, n) for n in range(1, fold)]
        for n in range(fold):
            places.append((chunk, n))
            last = len(places) == chunks * fold
            results.append(
                pair_update(
                    member,
                    places if last else places[-1:],
                    blocks[n],
                    rt,
                    weights,
                    vectors,
                    pair_state,
                    results if last else [],
                    width,
                )
            )
    return results[-1]


def solution(mesh):
    placed = (
        P("row", "col", None),
        P(),
        P(),
        P(),
        P(),
        P(),
        P(),
        P("row", "col", None),
        P(),
        P(),
        P(),
        P(),
        P(),
        P(),
    )

    return jax.shard_map(on_device, mesh=mesh, in_specs=placed, out_specs=P("row", "col", None), check_vma=False)
```
